256 devices in a mesh: series: 8 (over x, y_lo), tm: 32 (over z, y_hi, core).
Axes of the slice: x: 4, y: 4 (y_hi: 2, y_lo: 2; y = y_hi * 2 + y_lo), z: 8, core: 2. Of those that a mesh axis runs over, the one named last changes fastest.
Arguments:
- observed: bfloat16 [10240, 24576], P('series', 'tm'), may hold values from -6 to 6
- mask: int32 [10240, 24576], P('series', 'tm'), may hold values 0 or 1
- series_factors: float32 [10240, 256], P('series'), may hold values from -6 to 6
- time_factors: float32 [256, 24576], P(None, 'tm'), may hold values from -0.375 to 0.375
- ar_weights: float32 [3, 256], replicated, may hold values from -0.7 to 0.7
Outputs:
- series_out: float32 [10240, 256], P('series')
- time_out: float32 [256, 24576], P(None, 'tm')
- imputed: bfloat16 [10240, 24576], P('series', 'tm')
The draws below stay inside these ranges and needn't reach their ends.
Inputs may be any that keep to these rules, and one draw needn't show every extreme that they name: mask holds only 0 and 1.
All inputs are finite; a program needn't handle non-finite values. No bound on the sum of `mask` on one device may be relied on, other than what follows from the above.
Results may differ from the reference program's by a relative error of at most 0.0089.
Values sent between devices are 32-bit elements; how exact they have to be, the bound alone decides.
No kernel may reach another device: no remote copies, remote signals or barrier semaphores. Data moves between devices by JAX's collectives and lax.ppermute only.
A program may use at most 128 MiB of HBM per device.

```python
import jax
import jax.numpy as jnp
from jax import lax

K = 256
ITERS = 2
SERIES = 10240
HOURS = 24576


def plant(values, stream_key, smallest, largest):
    spot = [jax.random.randint(jax.random.fold_in(stream_key, axis), (), 0, length) for axis, length in enumerate(values.shape)]
    longest = values.shape.index(max(values.shape))
    neighbour = spot[:longest] + [(spot[longest] + 1) % values.shape[longest]] + spot[longest + 1:]
    return values.at[tuple(spot)].set(smallest).at[tuple(neighbour)].set(largest)


def block_scale(stream_key, dims, cuts, least, top_value):
    def one(axis_at, blocks):
        heights = jax.random.uniform(jax.random.fold_in(jax.random.fold_in(stream_key, 6), axis_at), (blocks,), jnp.float32, least / len(cuts), top_value / len(cuts))
        return jnp.repeat(jnp.exp(heights), dims[axis_at] // blocks).reshape((-1,) + (1,) * (len(dims) - axis_at - 1))

    loudness = one(*cuts[0])
    for cut in cuts[1:]:
        loudness = loudness * one(*cut)
    return loudness


def noise(stream_key, dims, deviation, reach, split=(), dtype=jnp.bfloat16):
    values = jax.random.normal(stream_key, dims, jnp.float32) * deviation
    if len(split) > 0:
        values = block_scale(stream_key, dims, split, -0.22, 0.18) * values
    return jnp.clip(values, min=-reach, max=reach).astype(dtype)


def setup_inputs(seed: int = 0) -> dict:
    streams_of = jax.random.split(jax.random.key(seed), 6)
    return {
        "observed": noise(streams_of[0], (SERIES, HOURS), 1.0, 6.0, ((0, 8), (1, 32))),
        "mask": plant((jax.random.randint(streams_of[1], (SERIES, HOURS), 0, 2) < 1).astype(jnp.int32), jax.random.fold_in(streams_of[1], 1), 0, 1),
        "series_factors": noise(streams_of[2], (SERIES, K), 1.0, 6.0, ((0, 8),), jnp.float32),
        "time_factors": noise(streams_of[3], (K, HOURS), K ** -0.5, 0.375, ((1, 32),), jnp.float32),
        "ar_weights": jnp.clip(jax.random.uniform(streams_of[4], (3, K), jnp.float32, -0.7, 0.7), -0.7, 0.7),
    }


lag_hours = (1, 24, 168)


def lag_terms(factors, weights):
    hour_count = factors.shape[1]
    in_range = jnp.arange(hour_count) >= 168
    lag_resid = factors
    for lag_index, lag_size in enumerate(lag_hours):
        earlier = jnp.pad(factors, ((0, 0), (lag_size, 0)))[:, :hour_count]
        lag_resid = lag_resid - weights[lag_index][:, None] * earlier
    lag_resid = jnp.where(in_range[None, :], lag_resid, jnp.zeros_like(lag_resid))
    backward = jnp.zeros_like(lag_resid)
    for lag_index, lag_size in enumerate(lag_hours):
        later = jnp.pad(lag_resid, ((0, 0), (0, lag_size)))[:, lag_size:]
        backward = backward + weights[lag_index][:, None] * later
    return lag_resid, backward


def reference(observed, mask, series_factors, time_factors, ar_weights):
    sensor_count, hour_count = observed.shape
    factor_rank = time_factors.shape[0]
    step_f = factor_rank / hour_count
    step_x = 1.0 / sensor_count
    ridge_f = 0.1 * hour_count / factor_rank
    ridge_x = 0.1 * sensor_count
    lam_ar = sensor_count / 8.0
    series_now = series_factors
    time_now = time_factors
    for sweep in range(ITERS):
        series_low = series_now.astype(jnp.bfloat16)
        time_low = time_now.astype(jnp.bfloat16)
        product = jnp.dot(series_low, time_low, preferred_element_type=jnp.float32)
        misfit = jnp.where(mask != 0, product - observed.astype(jnp.float32), jnp.zeros_like(product)).astype(jnp.bfloat16)
        grad_series = lax.dot_general(misfit, time_low, (((1,), (1,)), ((), ())), preferred_element_type=jnp.float32)
        grad_data = lax.dot_general(series_low, misfit, (((0,), (0,)), ((), ())), preferred_element_type=jnp.float32)
        lag_resid, backward = lag_terms(time_now, ar_weights)
        series_next = series_now - step_f * (grad_series + ridge_f * series_now)
        time_next = time_now - step_x * (grad_data + ridge_x * time_now + lam_ar * (lag_resid - backward))
        series_now, time_now = series_next, time_next
    imputed = jnp.dot(series_now.astype(jnp.bfloat16), time_now.astype(jnp.bfloat16), preferred_element_type=jnp.float32).astype(jnp.bfloat16)
    return series_now, time_now, imputed
```

```python
import jax
import jax.numpy as jnp
from jax import lax
from jax.sharding import Mesh
from jax.sharding import PartitionSpec as P

ITERS = 2
LAGS = (1, 24, 168)
EDGE = 168
SERIES = ("x", "y_lo")
FAR = ("z", "y_hi")
CORE = "core"
TM = (*FAR, CORE)
SWAP = ((0, 1), (1, 0))


def scattered_sum(array, axis):
    parts = array.reshape(lax.axis_size(axis), -1, array.shape[-1])
    return lax.all_to_all(parts, axis, 0, 0, tiled=True).sum(axis=0)


def gathered(array, axis):
    parts = jnp.broadcast_to(array[None], (lax.axis_size(axis), *array.shape))
    parts = lax.all_to_all(parts, axis, 0, 0, tiled=True)
    return parts.reshape(-1, array.shape[-1])


def passed_along(array, axis, by):
    length = lax.axis_size(axis)
    pairs = [(i, i + by) for i in range(length) if 0 <= i + by < length]
    return lax.ppermute(array, axis, pairs)


def lag_terms(now, weights, first, last):
    hours = now.shape[1]
    before = passed_along(now[:, hours - EDGE :], TM, 1)
    after = passed_along(now[:, :EDGE], TM, -1)
    wide = jnp.concatenate([before, now, after], axis=1)
    length = hours + EDGE
    resid = wide[:, EDGE:]
    for lag, weight in zip(LAGS, weights):
        resid = resid - weight[:, None] * wide[:, EDGE - lag : EDGE - lag + length]
    column = jnp.arange(length)
    inside = (~first | (column >= EDGE)) & (~last | (column < hours))
    resid = jnp.where(inside[None, :], resid, 0.0)
    back = None
    for lag, weight in zip(LAGS, weights):
        term = weight[:, None] * resid[:, lag : lag + hours]
        back = term if back is None else back + term
    return resid[:, :hours] - back


def local(observed, mask, series_factors, time_factors, ar_weights):
    rows, hours = observed.shape
    rank = time_factors.shape[0]
    hours_all = hours * lax.axis_size(TM)
    rows_all = rows * lax.axis_size(SERIES)
    step_f = rank / hours_all
    step_x = 1.0 / rows_all
    ridge_f = 0.1 * hours_all / rank
    ridge_x = 0.1 * rows_all
    lam = rows_all / 8.0

    half = rows // 2
    core = lax.axis_index(CORE)
    band = rank // lax.axis_size(SERIES)
    own_band = lax.axis_index(SERIES) * band
    place = lax.axis_index(TM)
    first, last = place == 0, place == lax.axis_size(TM) - 1

    keep = mask != 0
    wanted = observed.astype(jnp.float32)
    x_part = lax.dynamic_slice_in_dim(time_factors, own_band, band, 0)
    w_part = lax.dynamic_slice_in_dim(ar_weights, own_band, band, 1)
    f_full, x_full = series_factors, time_factors
    for _ in range(ITERS):
        f_low = f_full.astype(jnp.bfloat16)
        x_low = x_full.astype(jnp.bfloat16)
        product = jnp.dot(f_low, x_low, preferred_element_type=jnp.float32)
        misfit = jnp.where(keep, product - wanted, 0.0).astype(jnp.bfloat16)
        grad_f = lax.dot_general(
            misfit, x_low, (((1,), (1,)), ((), ())), preferred_element_type=jnp.float32
        )
        grad_x = lax.dot_general(
            f_low, misfit, (((0,), (0,)), ((), ())), preferred_element_type=jnp.float32
        )
        lag = lag_terms(x_part, w_part, first, last)
        theirs = lax.dynamic_slice_in_dim(grad_f, (1 - core) * half, half, 0)
        mine = lax.dynamic_slice_in_dim(grad_f, core * half, half, 0)
        mine = mine + lax.ppermute(theirs, CORE, SWAP)
        f_sum = scattered_sum(mine, FAR)
        x_sum = scattered_sum(grad_x, SERIES)
        x_push = x_sum + lam * lag
        x_part = x_part - step_x * (x_push + ridge_x * x_part)
        x_full = x_full - step_x * (gathered(x_push, SERIES) + ridge_x * x_full)
        mine = gathered(f_sum, FAR)
        theirs = lax.ppermute(mine, CORE, SWAP)
        f_sum = jnp.concatenate(
            [jnp.where(core == 0, mine, theirs), jnp.where(core == 0, theirs, mine)], axis=0
        )
        f_full = f_full - step_f * (f_sum + ridge_f * f_full)
    imputed = jnp.dot(
        f_full.astype(jnp.bfloat16), x_full.astype(jnp.bfloat16), preferred_element_type=jnp.float32
    ).astype(jnp.bfloat16)
    return f_full, x_full, imputed


def solution(mesh):
    far = mesh.shape["tm"] // 4
    near = mesh.shape["series"] // 2
    split = Mesh(
        mesh.devices.reshape(near, 2, far, 2, 2), (*SERIES, *TM)
    )
    in_specs = (P(SERIES, TM), P(SERIES, TM), P(SERIES, None), P(None, TM), P())
    out_specs = (P(SERIES, None), P(None, TM), P(SERIES, TM))
    return jax.shard_map(local, mesh=split, in_specs=in_specs, out_specs=out_specs, check_vma=False)
```

```python
import functools

import jax
import jax.numpy as jnp
from jax import lax
from jax.experimental import pallas as pl
from jax.experimental.pallas import tpu as pltpu
from jax.sharding import Mesh
from jax.sharding import PartitionSpec as P

ITERS = 2
LAGS = (1, 24, 168)
EDGE = 168
SERIES = ("x", "y_lo")
FAR = ("z", "y_hi")
CORE = "core"
TM = (*FAR, CORE)
SWAP = ((0, 1), (1, 0))
STEPS = 2
HIDDEN = 1e30
PARAMS = pltpu.CompilerParams(
    vmem_limit_bytes=20 * 2**20, dimension_semantics=("arbitrary",)
)
BF16, F32 = jnp.bfloat16, jnp.float32


def scattered_sum(array, axis):
    parts = array.reshape(lax.axis_size(axis), -1, array.shape[-1])
    return lax.all_to_all(parts, axis, 0, 0, tiled=True).sum(axis=0)


def gathered(array, axis):
    parts = jnp.broadcast_to(array[None], (lax.axis_size(axis), *array.shape))
    parts = lax.all_to_all(parts, axis, 0, 0, tiled=True)
    return parts.reshape(-1, array.shape[-1])


def traded(array, axis, bits):
    length = lax.axis_size(axis)
    return lax.ppermute(array, axis, [(i, i ^ bits) for i in range(length)])


def passed_along(array, axis, by):
    length = lax.axis_size(axis)
    pairs = [(i, i + by) for i in range(length) if 0 <= i + by < length]
    return lax.ppermute(array, axis, pairs)


def edges_of(now):
    return passed_along(now[:, -EDGE:], TM, 1), passed_along(now[:, :EDGE], TM, -1)


def lag_terms(now, edges, weights, first, last):
    before, after = edges
    hours = now.shape[1]
    wide = jnp.concatenate([before, now, after], axis=1)
    length = hours + EDGE
    resid = wide[:, EDGE:]
    for lag, weight in zip(LAGS, weights):
        resid = resid - weight[:, None] * wide[:, EDGE - lag : EDGE - lag + length]
    column = jnp.arange(length)
    inside = (~first | (column >= EDGE)) & (~last | (column < hours))
    resid = jnp.where(inside[None, :], resid, 0.0)
    back = None
    for lag, weight in zip(LAGS, weights):
        term = weight[:, None] * resid[:, lag : lag + hours]
        back = term if back is None else back + term
    return resid[:, :hours] - back


def natural(i, core):
    return ((i // STEPS + 1 + core) % 2) * STEPS + i % STEPS


def dot(a, b):
    return jnp.dot(a, b, preferred_element_type=F32)


def gradient(misfit, x_low, theirs_ref, mine_ref):
    grad = lax.dot_general(
        misfit, x_low, (((1,), (1,)), ((), ())), preferred_element_type=F32
    )

    @pl.when(pl.program_id(0) < STEPS)
    def _():
        theirs_ref[...] = grad

    @pl.when(pl.program_id(0) >= STEPS)
    def _():
        mine_ref[...] = grad


def first_pass(core_ref, x_ref, f_ref, seen_ref, mask_ref, theirs_ref, mine_ref, misfit_ref, f_low_ref, kept_ref, x_low_ref):
    @pl.when(pl.program_id(0) == 0)
    def _():
        x_low_ref[...] = x_ref[...].astype(BF16)

    x_low = x_low_ref[...]
    f_low = f_ref[...].astype(BF16)
    keep = mask_ref[...] != 0
    seen = seen_ref[...].astype(F32)
    misfit = jnp.where(keep, dot(f_low, x_low) - seen, 0.0).astype(BF16)
    kept_ref[...] = jnp.where(keep, seen, HIDDEN).astype(BF16)
    f_low_ref[...] = f_low
    misfit_ref[...] = misfit
    gradient(misfit, x_low, theirs_ref, mine_ref)


def assembled(along, pieces, *outs):
    for k, piece in enumerate(pieces):
        size = piece.shape[0]
        start = pl.multiple_of((along ^ k) * size, size)
        for out in outs:
            out[pl.ds(start, size), :] = piece[...].astype(out.dtype)


def later_pass(place_ref, *refs):
    *pieces, f_theirs_ref, f_mine_ref, kept_ref = refs[:-5]
    theirs_ref, mine_ref, misfit_ref, f_low_ref, x_low_ref = refs[-5:]

    @pl.when(pl.program_id(0) == 0)
    def _():
        assembled(place_ref[1], pieces, x_low_ref)

    x_low = x_low_ref[...]
    f_low = jnp.where(pl.program_id(0) < STEPS, f_theirs_ref[...], f_mine_ref[...]).astype(BF16)
    kept = kept_ref[...].astype(F32)
    misfit = jnp.where(kept < HIDDEN / 2, dot(f_low, x_low) - kept, 0.0).astype(BF16)
    f_low_ref[...] = f_low
    misfit_ref[...] = misfit
    gradient(misfit, x_low, theirs_ref, mine_ref)


def last_pass(place_ref, *refs):
    *pieces, f_theirs_ref, f_mine_ref = refs[:-4]
    f_ref, x_ref, imputed_ref, x_low_ref = refs[-4:]

    @pl.when(pl.program_id(0) == 0)
    def _():
        assembled(place_ref[1], pieces, x_low_ref, x_ref)

    f_now = jnp.where(pl.program_id(0) < STEPS, f_theirs_ref[...], f_mine_ref[...])
    f_ref[...] = f_now
    imputed_ref[...] = dot(f_now.astype(BF16), x_low_ref[...]).astype(BF16)


def row_pass(kernel, place, ins, outs, rank, hours, name):
    def spec(kind, shape):
        maps = {
            "whole": lambda i, p: (0, 0),
            "natural": lambda i, p: (natural(i, p[0]), 0),
            "step": lambda i, p: (i, 0),
            "theirs": lambda i, p: (jnp.minimum(i, STEPS - 1), 0),
            "mine": lambda i, p: (jnp.maximum(i - STEPS, 0), 0),
        }
        tiles = {"whole": 1, "theirs": STEPS, "mine": STEPS}.get(kind, 2 * STEPS)
        return pl.BlockSpec((shape[0] // tiles, shape[1]), maps[kind])

    rows = max(s.shape[0] for _, s in outs)
    moved = sum(a.size * a.dtype.itemsize for _, a in [*ins, *outs])
    return pl.pallas_call(
        kernel,
        out_shape=[s for _, s in outs],
        grid_spec=pltpu.PrefetchScalarGridSpec(
            num_scalar_prefetch=1,
            grid=(2 * STEPS,),
            in_specs=[spec(k, a.shape) for k, a in ins],
            out_specs=[spec(k, s.shape) for k, s in outs],
            scratch_shapes=[pltpu.VMEM((rank, hours), BF16)],
        ),
        compiler_params=PARAMS,
        cost_estimate=pl.CostEstimate(
            flops=4 * rows * rank * hours, bytes_accessed=moved, transcendentals=0
        ),
        name=name,
    )(place, *[a for _, a in ins])


def local(observed, mask, series_factors, time_factors, ar_weights):
    rows, hours = observed.shape
    rank = time_factors.shape[0]
    hours_all = hours * lax.axis_size(TM)
    rows_all = rows * lax.axis_size(SERIES)
    step_f = rank / hours_all
    step_x = 1.0 / rows_all
    ridge_f = 0.1 * hours_all / rank
    ridge_x = 0.1 * rows_all
    lam = rows_all / 8.0

    half = rows // 2
    core = lax.axis_index(CORE)
    line = half // lax.axis_size(FAR)
    own_row = core * half + lax.axis_index(FAR) * line
    peers = lax.axis_size("x")
    band = rank // peers
    along = lax.axis_index("x")
    position = lax.axis_index(TM)
    first, last = position == 0, position == lax.axis_size(TM) - 1
    place = jnp.stack([core, along])

    def shape(n, m, dtype=F32):
        return jax.ShapeDtypeStruct((n, m), dtype)

    grads = [
        ("theirs", shape(half, rank)),
        ("mine", shape(half, rank)),
        ("step", shape(rows, hours, BF16)),
        ("step", shape(rows, rank, BF16)),
    ]
    f_part = lax.dynamic_slice_in_dim(series_factors, own_row, line, 0)
    x_part = lax.dynamic_slice_in_dim(time_factors, along * band, band, 0)
    w_part = lax.dynamic_slice_in_dim(ar_weights, along * band, band, 1)
    for sweep in range(ITERS):
        if sweep == 0:
            theirs, mine, misfit, f_low, kept = row_pass(
                first_pass,
                place,
                [("whole", time_factors), ("natural", series_factors), ("natural", observed), ("natural", mask)],
                [*grads, ("step", shape(rows, hours, BF16))],
                rank,
                hours,
                "first_pass",
            )
        else:
            theirs, mine, misfit, f_low = row_pass(
                later_pass,
                place,
                [*[("whole", p) for p in pieces], ("theirs", f_theirs), ("mine", f_mine), ("step", kept)],
                grads,
                rank,
                hours,
                "later_pass",
            )
        mine = mine + lax.ppermute(theirs, CORE, SWAP)
        grad_x = lax.dot_general(
            f_low, misfit, (((0,), (0,)), ((), ())), preferred_element_type=F32
        )
        mine, grad_x, x_part = lax.optimization_barrier((mine, grad_x, x_part))
        if sweep == 0:
            edges = edges_of(x_part)
        f_sum = scattered_sum(mine, FAR)
        x_sum = lax.dynamic_slice_in_dim(grad_x, along * band, band, 0)
        for k in range(1, peers):
            part = lax.dynamic_slice_in_dim(grad_x, (along ^ k) * band, band, 0)
            x_sum = x_sum + traded(part, "x", k)
        x_sum = x_sum + lax.ppermute(x_sum, "y_lo", SWAP)
        lag = lag_terms(x_part, edges, w_part, first, last)
        f_part = f_part - step_f * (f_sum + ridge_f * f_part)
        x_part = x_part - step_x * (x_sum + ridge_x * x_part + lam * lag)
        f_part, x_part = lax.optimization_barrier((f_part, x_part))
        f_mine = gathered(f_part, FAR)
        pieces = [x_part] + [traded(x_part, "x", k) for k in range(1, peers)]
        if sweep + 1 < ITERS:
            edges = edges_of(x_part)
            f_mine, pieces, edges = lax.optimization_barrier((f_mine, pieces, edges))
        else:
            f_mine, pieces = lax.optimization_barrier((f_mine, pieces))
        f_theirs = lax.ppermute(f_mine, CORE, SWAP)
    return row_pass(
        last_pass,
        place,
        [*[("whole", p) for p in pieces], ("theirs", f_theirs), ("mine", f_mine)],
        [("natural", shape(rows, rank)), ("whole", shape(rank, hours)), ("natural", shape(rows, hours, BF16))],
        rank,
        hours,
        "last_pass",
    )


def solution(mesh):
    far = mesh.shape["tm"] // 4
    near = mesh.shape["series"] // 2
    split = Mesh(mesh.devices.reshape(near, 2, far, 2, 2), (*SERIES, *TM))
    in_specs = (P(SERIES, TM), P(SERIES, TM), P(SERIES, None), P(None, TM), P())
    out_specs = (P(SERIES, None), P(None, TM), P(SERIES, TM))
    return jax.shard_map(local, mesh=split, in_specs=in_specs, out_specs=out_specs, check_vma=False)
```

```python
import functools

import jax
import jax.numpy as jnp
from jax import lax
from jax.experimental import pallas as pl
from jax.experimental.pallas import tpu as pltpu
from jax.sharding import Mesh
from jax.sharding import PartitionSpec as P

ITERS = 2
LAGS = (1, 24, 168)
EDGE = 168
SERIES = ("x", "y_lo")
FAR = ("z", "y_hi")
CORE = "core"
TM = (*FAR, CORE)
SWAP = ((0, 1), (1, 0))
STEPS = 2
HIDDEN = 1e30
MIB = 2**20
BF16, F32 = jnp.bfloat16, jnp.float32


def scattered_sum(array, axis):
    parts = array.reshape(lax.axis_size(axis), -1, array.shape[-1])
    return lax.all_to_all(parts, axis, 0, 0, tiled=True).sum(axis=0)


def gathered(array, axis):
    parts = jnp.broadcast_to(array[None], (lax.axis_size(axis), *array.shape))
    parts = lax.all_to_all(parts, axis, 0, 0, tiled=True)
    return parts.reshape(-1, array.shape[-1])


def traded(array, axis, bits):
    length = lax.axis_size(axis)
    return lax.ppermute(array, axis, [(i, i ^ bits) for i in range(length)])


def passed_along(array, axis, by):
    length = lax.axis_size(axis)
    pairs = [(i, i + by) for i in range(length) if 0 <= i + by < length]
    return lax.ppermute(array, axis, pairs)


def edges_of(now):
    return passed_along(now[:, -EDGE:], TM, 1), passed_along(now[:, :EDGE], TM, -1)


def lag_terms(now, edges, weights, first, last):
    before, after = edges
    hours = now.shape[1]
    wide = jnp.concatenate([before, now, after], axis=1)
    length = hours + EDGE
    resid = wide[:, EDGE:]
    for lag, weight in zip(LAGS, weights):
        resid = resid - weight[:, None] * wide[:, EDGE - lag : EDGE - lag + length]
    column = jnp.arange(length)
    inside = (~first | (column >= EDGE)) & (~last | (column < hours))
    resid = jnp.where(inside[None, :], resid, 0.0)
    back = None
    for lag, weight in zip(LAGS, weights):
        term = weight[:, None] * resid[:, lag : lag + hours]
        back = term if back is None else back + term
    return resid[:, :hours] - back


def natural(i, core):
    return ((i // STEPS + 1 + core) % 2) * STEPS + i % STEPS


def dot(a, b):
    return jnp.dot(a, b, preferred_element_type=F32)


def gradients(misfit, f_low, x_low, along, theirs_ref, mine_ref, pieces, grad_x_ref):
    i = pl.program_id(0)
    grad_f = lax.dot_general(
        misfit, x_low, (((1,), (1,)), ((), ())), preferred_element_type=F32
    )
    grad_x = lax.dot_general(
        f_low, misfit, (((0,), (0,)), ((), ())), preferred_element_type=F32
    )

    @pl.when(i < STEPS)
    def _():
        theirs_ref[...] = grad_f

    @pl.when(i >= STEPS)
    def _():
        mine_ref[...] = grad_f

    @pl.when(i == 0)
    def _():
        grad_x_ref[...] = grad_x

    @pl.when(i > 0)
    def _():
        grad_x_ref[...] += grad_x

    @pl.when(i == 2 * STEPS - 1)
    def _():
        for k, piece in enumerate(pieces):
            size = piece.shape[0]
            start = pl.multiple_of((along ^ k) * size, size)
            piece[...] = grad_x_ref[pl.ds(start, size), :]


def first_pass(place_ref, x_ref, f_ref, seen_ref, mask_ref, *refs):
    theirs_ref, mine_ref, *pieces, kept_ref, x_low_ref, grad_x_ref = refs

    @pl.when(pl.program_id(0) == 0)
    def _():
        x_low_ref[...] = x_ref[...].astype(BF16)

    x_low = x_low_ref[...]
    f_low = f_ref[...].astype(BF16)
    keep = mask_ref[...] != 0
    seen = seen_ref[...].astype(F32)
    misfit = jnp.where(keep, dot(f_low, x_low) - seen, 0.0).astype(BF16)
    kept_ref[...] = jnp.where(keep, seen, HIDDEN).astype(BF16)
    gradients(misfit, f_low, x_low, place_ref[1], theirs_ref, mine_ref, pieces, grad_x_ref)


def assembled(along, pieces, *outs):
    for k, piece in enumerate(pieces):
        size = piece.shape[0]
        start = pl.multiple_of((along ^ k) * size, size)
        for out in outs:
            out[pl.ds(start, size), :] = piece[...].astype(out.dtype)


def later_pass(place_ref, *refs):
    count = (len(refs) - 7) // 2
    came, (f_theirs_ref, f_mine_ref, kept_ref) = refs[:count], refs[count : count + 3]
    theirs_ref, mine_ref, *pieces, x_low_ref, grad_x_ref = refs[count + 3 :]

    @pl.when(pl.program_id(0) == 0)
    def _():
        assembled(place_ref[1], came, x_low_ref)

    x_low = x_low_ref[...]
    f_low = jnp.where(pl.program_id(0) < STEPS, f_theirs_ref[...], f_mine_ref[...]).astype(BF16)
    kept = kept_ref[...].astype(F32)
    misfit = jnp.where(kept < HIDDEN / 2, dot(f_low, x_low) - kept, 0.0).astype(BF16)
    gradients(misfit, f_low, x_low, place_ref[1], theirs_ref, mine_ref, pieces, grad_x_ref)


def last_pass(place_ref, *refs):
    *pieces, f_theirs_ref, f_mine_ref = refs[:-4]
    f_ref, x_ref, imputed_ref, x_low_ref = refs[-4:]

    @pl.when(pl.program_id(0) == 0)
    def _():
        assembled(place_ref[1], pieces, x_low_ref, x_ref)

    f_now = jnp.where(pl.program_id(0) < STEPS, f_theirs_ref[...], f_mine_ref[...])
    f_ref[...] = f_now
    imputed_ref[...] = dot(f_now.astype(BF16), x_low_ref[...]).astype(BF16)


def row_pass(kernel, place, ins, outs, rank, hours, name, limit, scratch=()):
    def spec(kind, shape):
        maps = {
            "whole": lambda i, p: (0, 0),
            "natural": lambda i, p: (natural(i, p[0]), 0),
            "step": lambda i, p: (i, 0),
            "theirs": lambda i, p: (jnp.minimum(i, STEPS - 1), 0),
            "mine": lambda i, p: (jnp.maximum(i - STEPS, 0), 0),
        }
        tiles = {"whole": 1, "theirs": STEPS, "mine": STEPS}.get(kind, 2 * STEPS)
        return pl.BlockSpec((shape[0] // tiles, shape[1]), maps[kind])

    rows = max(s.shape[0] for _, s in outs)
    moved = sum(a.size * a.dtype.itemsize for _, a in [*ins, *outs])
    return pl.pallas_call(
        kernel,
        out_shape=[s for _, s in outs],
        grid_spec=pltpu.PrefetchScalarGridSpec(
            num_scalar_prefetch=1,
            grid=(2 * STEPS,),
            in_specs=[spec(k, a.shape) for k, a in ins],
            out_specs=[spec(k, s.shape) for k, s in outs],
            scratch_shapes=[pltpu.VMEM((rank, hours), BF16), *scratch],
        ),
        compiler_params=pltpu.CompilerParams(vmem_limit_bytes=limit * MIB),
        cost_estimate=pl.CostEstimate(
            flops=4 * rows * rank * hours, bytes_accessed=moved, transcendentals=0
        ),
        name=name,
    )(place, *[a for _, a in ins])


def local(observed, mask, series_factors, time_factors, ar_weights):
    rows, hours = observed.shape
    rank = time_factors.shape[0]
    hours_all = hours * lax.axis_size(TM)
    rows_all = rows * lax.axis_size(SERIES)
    step_f = rank / hours_all
    step_x = 1.0 / rows_all
    ridge_f = 0.1 * hours_all / rank
    ridge_x = 0.1 * rows_all
    lam = rows_all / 8.0

    half = rows // 2
    core = lax.axis_index(CORE)
    line = half // lax.axis_size(FAR)
    own_row = core * half + lax.axis_index(FAR) * line
    peers = lax.axis_size("x")
    band = rank // peers
    along = lax.axis_index("x")
    position = lax.axis_index(TM)
    first, last = position == 0, position == lax.axis_size(TM) - 1
    place = jnp.stack([core, along])

    def shape(n, m, dtype=F32):
        return jax.ShapeDtypeStruct((n, m), dtype)

    grads = [
        ("theirs", shape(half, rank)),
        ("mine", shape(half, rank)),
        *[("whole", shape(band, hours))] * peers,
    ]
    total = [pltpu.VMEM((rank, hours), F32)]
    f_part = lax.dynamic_slice_in_dim(series_factors, own_row, line, 0)
    x_part = lax.dynamic_slice_in_dim(time_factors, along * band, band, 0)
    w_part = lax.dynamic_slice_in_dim(ar_weights, along * band, band, 1)
    for sweep in range(ITERS):
        if sweep == 0:
            theirs, mine, *parts, kept = row_pass(
                first_pass,
                place,
                [("whole", time_factors), ("natural", series_factors), ("natural", observed), ("natural", mask)],
                [*grads, ("step", shape(rows, hours, BF16))],
                rank,
                hours,
                "first_pass",
                58,
                total,
            )
        else:
            theirs, mine, *parts = row_pass(
                later_pass,
                place,
                [*[("whole", p) for p in pieces], ("theirs", f_theirs), ("mine", f_mine), ("step", kept)],
                grads,
                rank,
                hours,
                "later_pass",
                20,
                total,
            )
        mine = mine + lax.ppermute(theirs, CORE, SWAP)
        mine, parts, x_part = lax.optimization_barrier((mine, parts, x_part))
        if sweep == 0:
            edges = edges_of(x_part)
        f_sum = scattered_sum(mine, FAR)
        x_sum = parts[0]
        for k in range(1, peers):
            x_sum = x_sum + traded(parts[k], "x", k)
        x_sum = x_sum + lax.ppermute(x_sum, "y_lo", SWAP)
        lag = lag_terms(x_part, edges, w_part, first, last)
        f_part = f_part - step_f * (f_sum + ridge_f * f_part)
        x_part = x_part - step_x * (x_sum + ridge_x * x_part + lam * lag)
        f_part, x_part = lax.optimization_barrier((f_part, x_part))
        f_mine = gathered(f_part, FAR)
        pieces = [x_part] + [traded(x_part, "x", k) for k in range(1, peers)]
        if sweep + 1 < ITERS:
            edges = edges_of(x_part)
            f_mine, pieces, edges = lax.optimization_barrier((f_mine, pieces, edges))
        else:
            f_mine, pieces = lax.optimization_barrier((f_mine, pieces))
        f_theirs = lax.ppermute(f_mine, CORE, SWAP)
    return row_pass(
        last_pass,
        place,
        [*[("whole", p) for p in pieces], ("theirs", f_theirs), ("mine", f_mine)],
        [("natural", shape(rows, rank)), ("whole", shape(rank, hours)), ("natural", shape(rows, hours, BF16))],
        rank,
        hours,
        "last_pass",
        20,
    )


def solution(mesh):
    far = mesh.shape["tm"] // 4
    near = mesh.shape["series"] // 2
    split = Mesh(mesh.devices.reshape(near, 2, far, 2, 2), (*SERIES, *TM))
    in_specs = (P(SERIES, TM), P(SERIES, TM), P(SERIES, None), P(None, TM), P())
    out_specs = (P(SERIES, None), P(None, TM), P(SERIES, TM))
    return jax.shard_map(local, mesh=split, in_specs=in_specs, out_specs=out_specs, check_vma=False)
```

```python
import functools

import jax
import jax.numpy as jnp
from jax import lax
from jax.experimental import pallas as pl
from jax.experimental.pallas import tpu as pltpu
from jax.sharding import Mesh
from jax.sharding import PartitionSpec as P

ITERS = 2
LAGS = (1, 24, 168)
EDGE = 168
SERIES = ("x", "y_lo")
FAR = ("z", "y_hi")
CORE = "core"
TM = (*FAR, CORE)
SWAP = ((0, 1), (1, 0))
STEPS = 2
HIDDEN = 1e30
BF16, F32 = jnp.bfloat16, jnp.float32


def scattered_sum(array, axis):
    parts = array.reshape(lax.axis_size(axis), -1, array.shape[-1])
    return lax.all_to_all(parts, axis, 0, 0, tiled=True).sum(axis=0)


def gathered(array, axis):
    parts = jnp.broadcast_to(array[None], (lax.axis_size(axis), *array.shape))
    parts = lax.all_to_all(parts, axis, 0, 0, tiled=True)
    return parts.reshape(-1, array.shape[-1])


def traded(array, axis, bits):
    length = lax.axis_size(axis)
    return lax.ppermute(array, axis, [(i, i ^ bits) for i in range(length)])


def passed_along(array, axis, by):
    length = lax.axis_size(axis)
    pairs = [(i, i + by) for i in range(length) if 0 <= i + by < length]
    return lax.ppermute(array, axis, pairs)


def edges_of(now):
    return passed_along(now[:, -EDGE:], TM, 1), passed_along(now[:, :EDGE], TM, -1)


def lag_terms(now, edges, weights, first, last):
    before, after = edges
    hours = now.shape[1]
    wide = jnp.concatenate([before, now, after], axis=1)
    length = hours + EDGE
    resid = wide[:, EDGE:]
    for lag, weight in zip(LAGS, weights):
        resid = resid - weight[:, None] * wide[:, EDGE - lag : EDGE - lag + length]
    column = jnp.arange(length)
    inside = (~first | (column >= EDGE)) & (~last | (column < hours))
    resid = jnp.where(inside[None, :], resid, 0.0)
    back = None
    for lag, weight in zip(LAGS, weights):
        term = weight[:, None] * resid[:, lag : lag + hours]
        back = term if back is None else back + term
    return resid[:, :hours] - back


def dot(a, b):
    return jnp.dot(a, b, preferred_element_type=F32)


def by_hours(misfit, x_low):
    return lax.dot_general(misfit, x_low, (((1,), (1,)), ((), ())), preferred_element_type=F32)


def by_rows(f_low, misfit):
    return lax.dot_general(f_low, misfit, (((0,), (0,)), ((), ())), preferred_element_type=F32)


def add_up(total_ref, term, start_ref=None):
    @pl.when(pl.program_id(0) == 0)
    def _():
        total_ref[...] = term if start_ref is None else start_ref[...] + term

    @pl.when(pl.program_id(0) > 0)
    def _():
        total_ref[...] += term


def share_out(along, total_ref, pieces):
    @pl.when(pl.program_id(0) == STEPS - 1)
    def _():
        for k, piece in enumerate(pieces):
            size = piece.shape[0]
            start = pl.multiple_of((along ^ k) * size, size)
            piece[...] = total_ref[pl.ds(start, size), :]


def assembled(along, pieces, *outs):
    @pl.when(pl.program_id(0) == 0)
    def _():
        for k, piece in enumerate(pieces):
            size = piece.shape[0]
            start = pl.multiple_of((along ^ k) * size, size)
            for out in outs:
                out[pl.ds(start, size), :] = piece[...].astype(out.dtype)


def first_half(x_ref, f_ref, seen_ref, mask_ref, grad_ref, kept_ref, x_low_ref):
    @pl.when(pl.program_id(0) == 0)
    def _():
        x_low_ref[...] = x_ref[...].astype(BF16)

    x_low = x_low_ref[...]
    f_low = f_ref[...].astype(BF16)
    keep = mask_ref[...] != 0
    seen = seen_ref[...].astype(F32)
    misfit = jnp.where(keep, dot(f_low, x_low) - seen, 0.0).astype(BF16)
    kept_ref[...] = jnp.where(keep, seen, HIDDEN).astype(BF16)
    grad_ref[...] = by_hours(misfit, x_low)
    return by_rows(f_low, misfit)


def first_theirs(_, x_ref, f_ref, seen_ref, mask_ref, grad_ref, kept_ref, total_ref, x_low_ref):
    add_up(total_ref, first_half(x_ref, f_ref, seen_ref, mask_ref, grad_ref, kept_ref, x_low_ref))


def first_mine(place_ref, x_ref, f_ref, seen_ref, mask_ref, start_ref, grad_ref, kept_ref, *refs):
    *pieces, x_low_ref, total_ref = refs
    term = first_half(x_ref, f_ref, seen_ref, mask_ref, grad_ref, kept_ref, x_low_ref)
    add_up(total_ref, term, start_ref)
    share_out(place_ref[1], total_ref, pieces)


def misfit_of(f_low, x_low, kept_ref):
    kept = kept_ref[...].astype(F32)
    return jnp.where(kept < HIDDEN / 2, dot(f_low, x_low) - kept, 0.0).astype(BF16)


def later_mine(place_ref, *refs):
    *came, f_ref, kept_ref, grad_ref, total_ref, x_low_ref = refs
    assembled(place_ref[1], came, x_low_ref)
    x_low = x_low_ref[...]
    f_low = f_ref[...].astype(BF16)
    misfit = misfit_of(f_low, x_low, kept_ref)
    grad_ref[...] = by_hours(misfit, x_low)
    add_up(total_ref, by_rows(f_low, misfit))


def later_theirs(_, x_low_ref, f_ref, kept_ref, grad_ref, misfit_ref):
    x_low = x_low_ref[...]
    misfit = misfit_of(f_ref[...].astype(BF16), x_low, kept_ref)
    misfit_ref[...] = misfit
    grad_ref[...] = by_hours(misfit, x_low)


def later_rows(place_ref, f_ref, misfit_ref, start_ref, *refs):
    *pieces, total_ref = refs
    add_up(total_ref, by_rows(f_ref[...].astype(BF16), misfit_ref[...]), start_ref)
    share_out(place_ref[1], total_ref, pieces)


def last_mine(place_ref, *refs):
    *came, f_ref, f_out_ref, imputed_ref, x_out_ref, x_low_ref = refs
    assembled(place_ref[1], came, x_out_ref, x_low_ref)
    f_out_ref[...] = f_ref[...]
    imputed_ref[...] = dot(f_ref[...].astype(BF16), x_low_ref[...]).astype(BF16)


def last_theirs(_, x_low_ref, f_ref, f_held_ref, imputed_held_ref, f_out_ref, imputed_ref):
    f_out_ref[...] = f_ref[...]
    imputed_ref[...] = dot(f_ref[...].astype(BF16), x_low_ref[...]).astype(BF16)


def half_pass(kernel, place, ins, outs, limit, matmuls, scratch=(), aliases=()):
    maps = {
        "whole": lambda i, p: (0, 0),
        "half": lambda i, p: (i, 0),
        "mine": lambda i, p: (p[0] * STEPS + i, 0),
        "theirs": lambda i, p: ((1 - p[0]) * STEPS + i, 0),
    }
    tiles = {"whole": 1, "half": STEPS, "mine": 2 * STEPS, "theirs": 2 * STEPS}

    def spec(kind, shape):
        if kind == "held":
            return pl.BlockSpec(memory_space=pl.ANY)
        return pl.BlockSpec((shape[0] // tiles[kind], shape[1]), maps[kind])

    moved = sum(
        a.size * a.dtype.itemsize // (2 if k in ("mine", "theirs") else 1)
        for k, a in [*ins, *outs]
        if k != "held"
    )
    work = max(a.size for _, a in [*ins, *outs]) * 256 // 2
    return pl.pallas_call(
        kernel,
        out_shape=[s for _, s in outs],
        grid_spec=pltpu.PrefetchScalarGridSpec(
            num_scalar_prefetch=1,
            grid=(STEPS,),
            in_specs=[spec(k, a.shape) for k, a in ins],
            out_specs=[spec(k, s.shape) for k, s in outs],
            scratch_shapes=list(scratch),
        ),
        compiler_params=pltpu.CompilerParams(vmem_limit_bytes=limit * 2**20),
        cost_estimate=pl.CostEstimate(
            flops=2 * matmuls * work, bytes_accessed=moved, transcendentals=0
        ),
        input_output_aliases=dict(aliases),
        name=kernel.__name__,
    )(place, *[a for _, a in ins])


def local(observed, mask, series_factors, time_factors, ar_weights):
    rows, hours = observed.shape
    rank = time_factors.shape[0]
    hours_all = hours * lax.axis_size(TM)
    rows_all = rows * lax.axis_size(SERIES)
    step_f = rank / hours_all
    step_x = 1.0 / rows_all
    ridge_f = 0.1 * hours_all / rank
    ridge_x = 0.1 * rows_all
    lam = rows_all / 8.0

    half = rows // 2
    core = lax.axis_index(CORE)
    line = half // lax.axis_size(FAR)
    own_row = core * half + lax.axis_index(FAR) * line
    peers = lax.axis_size("x")
    band = rank // peers
    along = lax.axis_index("x")
    position = lax.axis_index(TM)
    first, last = position == 0, position == lax.axis_size(TM) - 1
    place = jnp.stack([core, along])

    def shape(n, m, dtype=F32):
        return jax.ShapeDtypeStruct((n, m), dtype)

    grad = ("half", shape(half, rank))
    flags = ("half", shape(half, hours, BF16))
    total = ("whole", shape(rank, hours))
    low = ("whole", shape(rank, hours, BF16))
    shares = [("whole", shape(band, hours))] * peers
    total_scratch = pltpu.VMEM((rank, hours), F32)
    low_scratch = pltpu.VMEM((rank, hours), BF16)
    f_part = lax.dynamic_slice_in_dim(series_factors, own_row, line, 0)
    x_part = lax.dynamic_slice_in_dim(time_factors, along * band, band, 0)
    w_part = lax.dynamic_slice_in_dim(ar_weights, along * band, band, 1)
    for sweep in range(ITERS):
        if sweep == 0:
            theirs, kept_theirs, start = half_pass(
                first_theirs,
                place,
                [("whole", time_factors), ("theirs", series_factors), ("theirs", observed), ("theirs", mask)],
                [grad, flags, total],
                58,
                3,
                [low_scratch],
            )
            came = lax.ppermute(theirs, CORE, SWAP)
            mine, kept_mine, *parts = half_pass(
                first_mine,
                place,
                [("whole", time_factors), ("mine", series_factors), ("mine", observed), ("mine", mask), ("whole", start)],
                [grad, flags, *shares],
                58,
                3,
                [low_scratch, total_scratch],
            )
        else:
            mine, start, x_low = half_pass(
                later_mine,
                place,
                [*[("whole", p) for p in pieces], ("half", f_mine), ("half", kept_mine)],
                [grad, total, low],
                16,
                3,
            )
            theirs, misfit = half_pass(
                later_theirs,
                place,
                [("whole", x_low), ("half", f_theirs), ("half", kept_theirs)],
                [grad, flags],
                16,
                2,
            )
            came = lax.ppermute(theirs, CORE, SWAP)
            parts = half_pass(
                later_rows,
                place,
                [("half", f_theirs), ("half", misfit), ("whole", start)],
                shares,
                16,
                1,
                [total_scratch],
            )
        mine = mine + came
        mine, parts, x_part = lax.optimization_barrier((mine, parts, x_part))
        if sweep == 0:
            edges = edges_of(x_part)
        f_sum = scattered_sum(mine, FAR)
        x_sum = parts[0]
        for k in range(1, peers):
            x_sum = x_sum + traded(parts[k], "x", k)
        x_sum = x_sum + lax.ppermute(x_sum, "y_lo", SWAP)
        lag = lag_terms(x_part, edges, w_part, first, last)
        f_part = f_part - step_f * (f_sum + ridge_f * f_part)
        x_part = x_part - step_x * (x_sum + ridge_x * x_part + lam * lag)
        f_part, x_part = lax.optimization_barrier((f_part, x_part))
        f_mine = gathered(f_part, FAR)
        pieces = [x_part] + [traded(x_part, "x", k) for k in range(1, peers)]
        if sweep + 1 < ITERS:
            edges = edges_of(x_part)
            f_mine, pieces, edges = lax.optimization_barrier((f_mine, pieces, edges))
        else:
            f_mine, pieces = lax.optimization_barrier((f_mine, pieces))
        f_theirs = lax.ppermute(f_mine, CORE, SWAP)
    f_out, imputed, x_out, x_low = half_pass(
        last_mine,
        place,
        [*[("whole", p) for p in pieces], ("half", f_mine)],
        [("mine", shape(rows, rank)), ("mine", shape(rows, hours, BF16)), total, low],
        16,
        1,
    )
    f_out, imputed = half_pass(
        last_theirs,
        place,
        [("whole", x_low), ("half", f_theirs), ("held", f_out), ("held", imputed)],
        [("theirs", shape(rows, rank)), ("theirs", shape(rows, hours, BF16))],
        16,
        1,
        aliases={3: 0, 4: 1},
    )
    return f_out, x_out, imputed


def solution(mesh):
    far = mesh.shape["tm"] // 4
    near = mesh.shape["series"] // 2
    split = Mesh(mesh.devices.reshape(near, 2, far, 2, 2), (*SERIES, *TM))
    in_specs = (P(SERIES, TM), P(SERIES, TM), P(SERIES, None), P(None, TM), P())
    out_specs = (P(SERIES, None), P(None, TM), P(SERIES, TM))
    return jax.shard_map(local, mesh=split, in_specs=in_specs, out_specs=out_specs, check_vma=False)
```

```python
import functools

import jax
import jax.numpy as jnp
from jax import lax
from jax.experimental import pallas as pl
from jax.experimental.pallas import tpu as pltpu
from jax.sharding import Mesh
from jax.sharding import PartitionSpec as P

ITERS = 2
LAGS = (1, 24, 168)
EDGE = 168
SERIES = ("x", "y_lo")
FAR = ("z", "y_hi")
CORE = "core"
TM = (*FAR, CORE)
SWAP = ((0, 1), (1, 0))
FIRST, LATER = 5, 2
HIDDEN = 1e30
BF16, F32 = jnp.bfloat16, jnp.float32


def scattered_sum(array, axis):
    parts = array.reshape(lax.axis_size(axis), -1, array.shape[-1])
    return lax.all_to_all(parts, axis, 0, 0, tiled=True).sum(axis=0)


def gathered(array, axis):
    parts = jnp.broadcast_to(array[None], (lax.axis_size(axis), *array.shape))
    parts = lax.all_to_all(parts, axis, 0, 0, tiled=True)
    return parts.reshape(-1, array.shape[-1])


def traded(array, axis, bits):
    length = lax.axis_size(axis)
    return lax.ppermute(array, axis, [(i, i ^ bits) for i in range(length)])


def passed_along(array, axis, by):
    length = lax.axis_size(axis)
    pairs = [(i, i + by) for i in range(length) if 0 <= i + by < length]
    return lax.ppermute(array, axis, pairs)


def edges_of(now):
    return passed_along(now[:, -EDGE:], TM, 1), passed_along(now[:, :EDGE], TM, -1)


def lag_terms(now, edges, weights, first, last):
    before, after = edges
    hours = now.shape[1]
    wide = jnp.concatenate([before, now, after], axis=1)
    length = hours + EDGE
    resid = wide[:, EDGE:]
    for lag, weight in zip(LAGS, weights):
        resid = resid - weight[:, None] * wide[:, EDGE - lag : EDGE - lag + length]
    column = jnp.arange(length)
    inside = (~first | (column >= EDGE)) & (~last | (column < hours))
    resid = jnp.where(inside[None, :], resid, 0.0)
    back = None
    for lag, weight in zip(LAGS, weights):
        term = weight[:, None] * resid[:, lag : lag + hours]
        back = term if back is None else back + term
    return resid[:, :hours] - back


def dot(a, b):
    return jnp.dot(a, b, preferred_element_type=F32)


def by_hours(misfit, x_low):
    return lax.dot_general(misfit, x_low, (((1,), (1,)), ((), ())), preferred_element_type=F32)


def by_rows(f_low, misfit):
    return lax.dot_general(f_low, misfit, (((0,), (0,)), ((), ())), preferred_element_type=F32)


def add_up(total_ref, term, start_ref=None):
    @pl.when(pl.program_id(0) == 0)
    def _():
        total_ref[...] = term if start_ref is None else start_ref[...] + term

    @pl.when(pl.program_id(0) > 0)
    def _():
        total_ref[...] += term


def share_out(along, total_ref, pieces):
    @pl.when(pl.program_id(0) == pl.num_programs(0) - 1)
    def _():
        for k, piece in enumerate(pieces):
            size = piece.shape[0]
            start = pl.multiple_of((along ^ k) * size, size)
            piece[...] = total_ref[pl.ds(start, size), :]


def assembled(along, pieces, *outs):
    @pl.when(pl.program_id(0) == 0)
    def _():
        for k, piece in enumerate(pieces):
            size = piece.shape[0]
            start = pl.multiple_of((along ^ k) * size, size)
            for out in outs:
                out[pl.ds(start, size), :] = piece[...].astype(out.dtype)


def first_half(x_ref, f_ref, seen_ref, mask_ref, grad_ref, kept_ref, x_low_ref):
    @pl.when(pl.program_id(0) == 0)
    def _():
        x_low_ref[...] = x_ref[...].astype(BF16)

    x_low = x_low_ref[...]
    f_low = f_ref[...].astype(BF16)
    keep = mask_ref[...] != 0
    seen = seen_ref[...].astype(F32)
    misfit = jnp.where(keep, dot(f_low, x_low) - seen, 0.0).astype(BF16)
    kept_ref[...] = jnp.where(keep, seen, HIDDEN).astype(BF16)
    grad_ref[...] = by_hours(misfit, x_low)
    return by_rows(f_low, misfit)


def first_theirs(_, x_ref, f_ref, seen_ref, mask_ref, grad_ref, kept_ref, total_ref, x_low_ref):
    add_up(total_ref, first_half(x_ref, f_ref, seen_ref, mask_ref, grad_ref, kept_ref, x_low_ref))


def first_mine(place_ref, x_ref, f_ref, seen_ref, mask_ref, start_ref, grad_ref, kept_ref, *refs):
    *pieces, x_part_ref, x_low_ref, total_ref = refs
    size = x_part_ref.shape[0]

    @pl.when(pl.program_id(0) == 0)
    def _():
        x_part_ref[...] = x_ref[pl.ds(pl.multiple_of(place_ref[1] * size, size), size), :]

    term = first_half(x_ref, f_ref, seen_ref, mask_ref, grad_ref, kept_ref, x_low_ref)
    add_up(total_ref, term, start_ref)
    share_out(place_ref[1], total_ref, pieces)


def misfit_of(f_low, x_low, kept_ref):
    kept = kept_ref[...].astype(F32)
    return jnp.where(kept < HIDDEN / 2, dot(f_low, x_low) - kept, 0.0).astype(BF16)


def later_mine(place_ref, *refs):
    *came, f_ref, kept_ref, grad_ref, total_ref, x_low_ref = refs
    assembled(place_ref[1], came, x_low_ref)
    x_low = x_low_ref[...]
    f_low = f_ref[...].astype(BF16)
    misfit = misfit_of(f_low, x_low, kept_ref)
    grad_ref[...] = by_hours(misfit, x_low)
    add_up(total_ref, by_rows(f_low, misfit))


def later_theirs(_, x_low_ref, f_ref, kept_ref, grad_ref, misfit_ref):
    x_low = x_low_ref[...]
    misfit = misfit_of(f_ref[...].astype(BF16), x_low, kept_ref)
    misfit_ref[...] = misfit
    grad_ref[...] = by_hours(misfit, x_low)


def later_rows(place_ref, f_ref, misfit_ref, start_ref, *refs):
    *pieces, total_ref = refs
    add_up(total_ref, by_rows(f_ref[...].astype(BF16), misfit_ref[...]), start_ref)
    share_out(place_ref[1], total_ref, pieces)


def last_mine(place_ref, *refs):
    *came, f_ref, f_out_ref, imputed_ref, x_out_ref, x_low_ref = refs
    assembled(place_ref[1], came, x_out_ref, x_low_ref)
    f_out_ref[...] = f_ref[...]
    imputed_ref[...] = dot(f_ref[...].astype(BF16), x_low_ref[...]).astype(BF16)


def last_theirs(_, x_low_ref, f_ref, f_held_ref, imputed_held_ref, f_out_ref, imputed_ref):
    f_out_ref[...] = f_ref[...]
    imputed_ref[...] = dot(f_ref[...].astype(BF16), x_low_ref[...]).astype(BF16)


def half_pass(kernel, place, ins, outs, steps, limit, matmuls, scratch=(), aliases=()):
    maps = {
        "whole": lambda i, p: (0, 0),
        "half": lambda i, p: (i, 0),
        "mine": lambda i, p: (p[0] * steps + i, 0),
        "theirs": lambda i, p: ((1 - p[0]) * steps + i, 0),
    }
    tiles = {"whole": 1, "half": steps, "mine": 2 * steps, "theirs": 2 * steps}

    def spec(kind, shape):
        if kind == "held":
            return pl.BlockSpec(memory_space=pl.ANY)
        return pl.BlockSpec((shape[0] // tiles[kind], shape[1]), maps[kind])

    moved = sum(
        a.size * a.dtype.itemsize // (2 if k in ("mine", "theirs") else 1)
        for k, a in [*ins, *outs]
        if k != "held"
    )
    work = max(a.size for _, a in [*ins, *outs]) * 256 // 2
    return pl.pallas_call(
        kernel,
        out_shape=[s for _, s in outs],
        grid_spec=pltpu.PrefetchScalarGridSpec(
            num_scalar_prefetch=1,
            grid=(steps,),
            in_specs=[spec(k, a.shape) for k, a in ins],
            out_specs=[spec(k, s.shape) for k, s in outs],
            scratch_shapes=list(scratch),
        ),
        compiler_params=pltpu.CompilerParams(vmem_limit_bytes=limit * 2**20),
        cost_estimate=pl.CostEstimate(
            flops=2 * matmuls * work, bytes_accessed=moved, transcendentals=0
        ),
        input_output_aliases=dict(aliases),
        name=kernel.__name__,
    )(place, *[a for _, a in ins])


def local(observed, mask, series_factors, time_factors, ar_weights):
    rows, hours = observed.shape
    rank = time_factors.shape[0]
    hours_all = hours * lax.axis_size(TM)
    rows_all = rows * lax.axis_size(SERIES)
    step_f = rank / hours_all
    step_x = 1.0 / rows_all
    ridge_f = 0.1 * hours_all / rank
    ridge_x = 0.1 * rows_all
    lam = rows_all / 8.0

    half = rows // 2
    core = lax.axis_index(CORE)
    line = half // lax.axis_size(FAR)
    own_row = core * half + lax.axis_index(FAR) * line
    peers = lax.axis_size("x")
    band = rank // peers
    along = lax.axis_index("x")
    position = lax.axis_index(TM)
    first, last = position == 0, position == lax.axis_size(TM) - 1
    place = jnp.stack([core, along])

    def shape(n, m, dtype=F32):
        return jax.ShapeDtypeStruct((n, m), dtype)

    grad = ("half", shape(half, rank))
    flags = ("half", shape(half, hours, BF16))
    total = ("whole", shape(rank, hours))
    low = ("whole", shape(rank, hours, BF16))
    shares = [("whole", shape(band, hours))] * peers
    total_scratch = pltpu.VMEM((rank, hours), F32)
    low_scratch = pltpu.VMEM((rank, hours), BF16)
    f_part = lax.dynamic_slice_in_dim(series_factors, own_row, line, 0)
    w_part = lax.dynamic_slice_in_dim(ar_weights, along * band, band, 1)
    for sweep in range(ITERS):
        if sweep == 0:
            theirs, kept_theirs, start = half_pass(
                first_theirs,
                place,
                [("whole", time_factors), ("theirs", series_factors), ("theirs", observed), ("theirs", mask)],
                [grad, flags, total],
                FIRST,
                58,
                3,
                [low_scratch],
            )
            came = lax.ppermute(theirs, CORE, SWAP)
            mine, kept_mine, *parts, x_part = half_pass(
                first_mine,
                place,
                [("whole", time_factors), ("mine", series_factors), ("mine", observed), ("mine", mask), ("whole", start)],
                [grad, flags, *shares, shares[0]],
                FIRST,
                58,
                3,
                [low_scratch, total_scratch],
            )
        else:
            mine, start, x_low = half_pass(
                later_mine,
                place,
                [*[("whole", p) for p in pieces], ("half", f_mine), ("half", kept_mine)],
                [grad, total, low],
                LATER,
                16,
                3,
            )
            theirs, misfit = half_pass(
                later_theirs,
                place,
                [("whole", x_low), ("half", f_theirs), ("half", kept_theirs)],
                [grad, flags],
                LATER,
                16,
                2,
            )
            came = lax.ppermute(theirs, CORE, SWAP)
            parts = half_pass(
                later_rows,
                place,
                [("half", f_theirs), ("half", misfit), ("whole", start)],
                shares,
                LATER,
                16,
                1,
                [total_scratch],
            )
        mine = mine + came
        mine, parts, x_part = lax.optimization_barrier((mine, parts, x_part))
        edges = edges_of(x_part)
        f_sum = scattered_sum(mine, FAR)
        x_sum = parts[0]
        for k in range(1, peers):
            x_sum = x_sum + traded(parts[k], "x", k)
        lag = lag_terms(x_part, edges, w_part, first, last)
        f_part, x_sum, lag = lax.optimization_barrier((f_part, x_sum, lag))
        f_part = f_part - step_f * (f_sum + ridge_f * f_part)
        x_sum = x_sum + lax.ppermute(x_sum, "y_lo", SWAP)
        x_part = x_part - step_x * (x_sum + ridge_x * x_part + lam * lag)
        f_mine = gathered(f_part, FAR)
        pieces = [x_part] + [traded(x_part, "x", k) for k in range(1, peers)]
        f_mine, pieces = lax.optimization_barrier((f_mine, pieces))
        f_theirs = lax.ppermute(f_mine, CORE, SWAP)
    f_out, imputed, x_out, x_low = half_pass(
        last_mine,
        place,
        [*[("whole", p) for p in pieces], ("half", f_mine)],
        [("mine", shape(rows, rank)), ("mine", shape(rows, hours, BF16)), total, low],
        LATER,
        16,
        1,
    )
    f_out, imputed = half_pass(
        last_theirs,
        place,
        [("whole", x_low), ("half", f_theirs), ("held", f_out), ("held", imputed)],
        [("theirs", shape(rows, rank)), ("theirs", shape(rows, hours, BF16))],
        LATER,
        16,
        1,
        aliases={3: 0, 4: 1},
    )
    return f_out, x_out, imputed


def solution(mesh):
    far = mesh.shape["tm"] // 4
    near = mesh.shape["series"] // 2
    split = Mesh(mesh.devices.reshape(near, 2, far, 2, 2), (*SERIES, *TM))
    in_specs = (P(SERIES, TM), P(SERIES, TM), P(SERIES, None), P(None, TM), P())
    out_specs = (P(SERIES, None), P(None, TM), P(SERIES, TM))
    return jax.shard_map(local, mesh=split, in_specs=in_specs, out_specs=out_specs, check_vma=False)
```

```python
import functools

import jax
import jax.numpy as jnp
from jax import lax
from jax.experimental import pallas as pl
from jax.experimental.pallas import tpu as pltpu
from jax.sharding import Mesh
from jax.sharding import PartitionSpec as P

ITERS = 2
LAGS = (1, 24, 168)
EDGE = 168
SERIES = ("x", "y_lo")
FAR = ("z", "y_hi")
CORE = "core"
TM = (*FAR, CORE)
SWAP = ((0, 1), (1, 0))
FIRST, LATER = 2, 2
HIDDEN = 1e30
BF16, F32 = jnp.bfloat16, jnp.float32


def scattered_sum(array, axis):
    parts = array.reshape(lax.axis_size(axis), -1, array.shape[-1])
    return lax.all_to_all(parts, axis, 0, 0, tiled=True).sum(axis=0)


def gathered(array, axis):
    parts = jnp.broadcast_to(array[None], (lax.axis_size(axis), *array.shape))
    parts = lax.all_to_all(parts, axis, 0, 0, tiled=True)
    return parts.reshape(-1, array.shape[-1])


def traded(array, axis, bits):
    length = lax.axis_size(axis)
    return lax.ppermute(array, axis, [(i, i ^ bits) for i in range(length)])


def passed_along(array, axis, by):
    length = lax.axis_size(axis)
    pairs = [(i, i + by) for i in range(length) if 0 <= i + by < length]
    return lax.ppermute(array, axis, pairs)


def edges_of(now):
    return passed_along(now[:, -EDGE:], TM, 1), passed_along(now[:, :EDGE], TM, -1)


def lag_terms(now, edges, weights, first, last):
    before, after = edges
    hours = now.shape[1]
    wide = jnp.concatenate([before, now, after], axis=1)
    length = hours + EDGE
    resid = wide[:, EDGE:]
    for lag, weight in zip(LAGS, weights):
        resid = resid - weight[:, None] * wide[:, EDGE - lag : EDGE - lag + length]
    column = jnp.arange(length)
    inside = (~first | (column >= EDGE)) & (~last | (column < hours))
    resid = jnp.where(inside[None, :], resid, 0.0)
    back = None
    for lag, weight in zip(LAGS, weights):
        term = weight[:, None] * resid[:, lag : lag + hours]
        back = term if back is None else back + term
    return resid[:, :hours] - back


def dot(a, b):
    return jnp.dot(a, b, preferred_element_type=F32)


def by_hours(misfit, x_low):
    return lax.dot_general(misfit, x_low, (((1,), (1,)), ((), ())), preferred_element_type=F32)


def by_rows(f_low, misfit):
    return lax.dot_general(f_low, misfit, (((0,), (0,)), ((), ())), preferred_element_type=F32)


def add_up(total_ref, term, start_ref=None):
    @pl.when(pl.program_id(0) == 0)
    def _():
        total_ref[...] = term if start_ref is None else start_ref[...] + term

    @pl.when(pl.program_id(0) > 0)
    def _():
        total_ref[...] += term


def share_out(along, total_ref, pieces):
    @pl.when(pl.program_id(0) == pl.num_programs(0) - 1)
    def _():
        for k, piece in enumerate(pieces):
            size = piece.shape[0]
            start = pl.multiple_of((along ^ k) * size, size)
            piece[...] = total_ref[pl.ds(start, size), :]


def assembled(along, pieces, *outs):
    @pl.when(pl.program_id(0) == 0)
    def _():
        for k, piece in enumerate(pieces):
            size = piece.shape[0]
            start = pl.multiple_of((along ^ k) * size, size)
            for out in outs:
                out[pl.ds(start, size), :] = piece[...].astype(out.dtype)


def first_pass(place_ref, x_ref, f_ref, seen_ref, mask_ref, *refs):
    halves, (*pieces, x_part_ref, x_low_ref, total_ref) = refs[:4], refs[4:]
    i = pl.program_id(0)

    @pl.when(i == 0)
    def _():
        size = x_part_ref.shape[0]
        x_low_ref[...] = x_ref[...].astype(BF16)
        x_part_ref[...] = x_ref[pl.ds(pl.multiple_of(place_ref[1] * size, size), size), :]

    x_low = x_low_ref[...]
    f_low = f_ref[...].astype(BF16)
    keep = mask_ref[...] != 0
    seen = seen_ref[...].astype(F32)
    misfit = jnp.where(keep, dot(f_low, x_low) - seen, 0.0).astype(BF16)
    kept = jnp.where(keep, seen, HIDDEN).astype(BF16)
    grad = by_hours(misfit, x_low)

    @pl.when(i < FIRST)
    def _():
        halves[0][...] = grad
        halves[2][...] = kept

    @pl.when(i >= FIRST)
    def _():
        halves[1][...] = grad
        halves[3][...] = kept

    add_up(total_ref, by_rows(f_low, misfit))
    share_out(place_ref[1], total_ref, pieces)


def misfit_of(f_low, x_low, kept_ref):
    kept = kept_ref[...].astype(F32)
    return jnp.where(kept < HIDDEN / 2, dot(f_low, x_low) - kept, 0.0).astype(BF16)


def later_mine(place_ref, *refs):
    *came, f_ref, kept_ref, grad_ref, total_ref, x_low_ref = refs
    assembled(place_ref[1], came, x_low_ref)
    x_low = x_low_ref[...]
    f_low = f_ref[...].astype(BF16)
    misfit = misfit_of(f_low, x_low, kept_ref)
    grad_ref[...] = by_hours(misfit, x_low)
    add_up(total_ref, by_rows(f_low, misfit))


def later_theirs(_, x_low_ref, f_ref, kept_ref, grad_ref, misfit_ref):
    x_low = x_low_ref[...]
    misfit = misfit_of(f_ref[...].astype(BF16), x_low, kept_ref)
    misfit_ref[...] = misfit
    grad_ref[...] = by_hours(misfit, x_low)


def later_rows(place_ref, f_ref, misfit_ref, start_ref, *refs):
    *pieces, total_ref = refs
    add_up(total_ref, by_rows(f_ref[...].astype(BF16), misfit_ref[...]), start_ref)
    share_out(place_ref[1], total_ref, pieces)


def last_mine(place_ref, *refs):
    *came, f_ref, f_out_ref, imputed_ref, x_out_ref, x_low_ref = refs
    assembled(place_ref[1], came, x_out_ref, x_low_ref)
    f_out_ref[...] = f_ref[...]
    imputed_ref[...] = dot(f_ref[...].astype(BF16), x_low_ref[...]).astype(BF16)


def last_theirs(_, x_low_ref, f_ref, f_held_ref, imputed_held_ref, f_out_ref, imputed_ref):
    f_out_ref[...] = f_ref[...]
    imputed_ref[...] = dot(f_ref[...].astype(BF16), x_low_ref[...]).astype(BF16)


def half_pass(kernel, place, ins, outs, steps, limit, matmuls, scratch=(), aliases=()):
    maps = {
        "whole": lambda i, p: (0, 0),
        "half": lambda i, p: (i, 0),
        "mine": lambda i, p: (p[0] * steps + i, 0),
        "theirs": lambda i, p: ((1 - p[0]) * steps + i, 0),
        "both": lambda i, p: ((i // FIRST + 1 + p[0]) % 2 * FIRST + i % FIRST, 0),
        "former": lambda i, p: (jnp.minimum(i, FIRST - 1), 0),
        "latter": lambda i, p: (jnp.maximum(i - FIRST, 0), 0),
    }
    tiles = {"whole": 1, "half": steps, "mine": 2 * steps, "theirs": 2 * steps}
    tiles.update(both=2 * FIRST, former=FIRST, latter=FIRST)

    def spec(kind, shape):
        if kind == "held":
            return pl.BlockSpec(memory_space=pl.ANY)
        return pl.BlockSpec((shape[0] // tiles[kind], shape[1]), maps[kind])

    moved = sum(
        a.size * a.dtype.itemsize // (2 if k in ("mine", "theirs") else 1)
        for k, a in [*ins, *outs]
        if k != "held"
    )
    work = max(a.size for _, a in [*ins, *outs]) * 256 // 2
    return pl.pallas_call(
        kernel,
        out_shape=[s for _, s in outs],
        grid_spec=pltpu.PrefetchScalarGridSpec(
            num_scalar_prefetch=1,
            grid=(steps,),
            in_specs=[spec(k, a.shape) for k, a in ins],
            out_specs=[spec(k, s.shape) for k, s in outs],
            scratch_shapes=list(scratch),
        ),
        compiler_params=pltpu.CompilerParams(vmem_limit_bytes=limit * 2**20),
        cost_estimate=pl.CostEstimate(
            flops=2 * matmuls * work, bytes_accessed=moved, transcendentals=0
        ),
        input_output_aliases=dict(aliases),
        name=kernel.__name__,
    )(place, *[a for _, a in ins])


def local(observed, mask, series_factors, time_factors, ar_weights):
    rows, hours = observed.shape
    rank = time_factors.shape[0]
    hours_all = hours * lax.axis_size(TM)
    rows_all = rows * lax.axis_size(SERIES)
    step_f = rank / hours_all
    step_x = 1.0 / rows_all
    ridge_f = 0.1 * hours_all / rank
    ridge_x = 0.1 * rows_all
    lam = rows_all / 8.0

    half = rows // 2
    core = lax.axis_index(CORE)
    line = half // lax.axis_size(FAR)
    own_row = core * half + lax.axis_index(FAR) * line
    peers = lax.axis_size("x")
    band = rank // peers
    along = lax.axis_index("x")
    position = lax.axis_index(TM)
    first, last = position == 0, position == lax.axis_size(TM) - 1
    place = jnp.stack([core, along])

    def shape(n, m, dtype=F32):
        return jax.ShapeDtypeStruct((n, m), dtype)

    grad = ("half", shape(half, rank))
    flags = ("half", shape(half, hours, BF16))
    total = ("whole", shape(rank, hours))
    low = ("whole", shape(rank, hours, BF16))
    shares = [("whole", shape(band, hours))] * peers
    total_scratch = pltpu.VMEM((rank, hours), F32)
    low_scratch = pltpu.VMEM((rank, hours), BF16)
    f_part = lax.dynamic_slice_in_dim(series_factors, own_row, line, 0)
    w_part = lax.dynamic_slice_in_dim(ar_weights, along * band, band, 1)
    for sweep in range(ITERS):
        if sweep == 0:
            theirs, mine, kept_theirs, kept_mine, *parts, x_part = half_pass(
                first_pass,
                place,
                [("whole", time_factors), ("both", series_factors), ("both", observed), ("both", mask)],
                [("former", grad[1]), ("latter", grad[1]), ("former", flags[1]), ("latter", flags[1]), *shares, shares[0]],
                2 * FIRST,
                58,
                6,
                [low_scratch, total_scratch],
            )
            came = lax.ppermute(theirs, CORE, SWAP)
        else:
            mine, start, x_low = half_pass(
                later_mine,
                place,
                [*[("whole", p) for p in pieces], ("half", f_mine), ("half", kept_mine)],
                [grad, total, low],
                LATER,
                16,
                3,
            )
            theirs, misfit = half_pass(
                later_theirs,
                place,
                [("whole", x_low), ("half", f_theirs), ("half", kept_theirs)],
                [grad, flags],
                LATER,
                16,
                2,
            )
            came = lax.ppermute(theirs, CORE, SWAP)
            parts = half_pass(
                later_rows,
                place,
                [("half", f_theirs), ("half", misfit), ("whole", start)],
                shares,
                LATER,
                16,
                1,
                [total_scratch],
            )
        mine = mine + came
        mine, parts, x_part = lax.optimization_barrier((mine, parts, x_part))
        f_sum = scattered_sum(mine, FAR)
        received = [traded(parts[k], "x", k) for k in range(1, peers)]
        edge_x, received[0] = lax.optimization_barrier((x_part, received[0]))
        edges = edges_of(edge_x)
        x_sum = parts[0]
        for part in received:
            x_sum = x_sum + part
        lag = lag_terms(x_part, edges, w_part, first, last)
        f_part, x_sum, lag = lax.optimization_barrier((f_part, x_sum, lag))
        f_part = f_part - step_f * (f_sum + ridge_f * f_part)
        x_sum = x_sum + lax.ppermute(x_sum, "y_lo", SWAP)
        x_part = x_part - step_x * (x_sum + ridge_x * x_part + lam * lag)
        f_mine = gathered(f_part, FAR)
        pieces = [x_part] + [traded(x_part, "x", k) for k in range(1, peers)]
        f_mine, pieces = lax.optimization_barrier((f_mine, pieces))
        f_theirs = lax.ppermute(f_mine, CORE, SWAP)
    f_out, imputed, x_out, x_low = half_pass(
        last_mine,
        place,
        [*[("whole", p) for p in pieces], ("half", f_mine)],
        [("mine", shape(rows, rank)), ("mine", shape(rows, hours, BF16)), total, low],
        LATER,
        16,
        1,
    )
    f_out, imputed = half_pass(
        last_theirs,
        place,
        [("whole", x_low), ("half", f_theirs), ("held", f_out), ("held", imputed)],
        [("theirs", shape(rows, rank)), ("theirs", shape(rows, hours, BF16))],
        LATER,
        16,
        1,
        aliases={3: 0, 4: 1},
    )
    return f_out, x_out, imputed


def solution(mesh):
    far = mesh.shape["tm"] // 4
    near = mesh.shape["series"] // 2
    split = Mesh(mesh.devices.reshape(near, 2, far, 2, 2), (*SERIES, *TM))
    in_specs = (P(SERIES, TM), P(SERIES, TM), P(SERIES, None), P(None, TM), P())
    out_specs = (P(SERIES, None), P(None, TM), P(SERIES, TM))
    return jax.shard_map(local, mesh=split, in_specs=in_specs, out_specs=out_specs, check_vma=False)
```

```python
import functools

import jax
import jax.numpy as jnp
from jax import lax
from jax.experimental import pallas as pl
from jax.experimental.pallas import tpu as pltpu
from jax.sharding import Mesh
from jax.sharding import PartitionSpec as P

ITERS = 2
LAGS = (1, 24, 168)
EDGE = 168
SERIES = ("x", "y_lo")
FAR = ("z", "y_hi")
CORE = "core"
TM = (*FAR, CORE)
SWAP = ((0, 1), (1, 0))
FIRST, LATER, LAST = 2, 1, 2
HIDDEN = 1e30
BF16, F32 = jnp.bfloat16, jnp.float32


def scattered_sum(array, axis):
    parts = array.reshape(lax.axis_size(axis), -1, array.shape[-1])
    return lax.all_to_all(parts, axis, 0, 0, tiled=True).sum(axis=0)


def gathered(array, axis):
    parts = jnp.broadcast_to(array[None], (lax.axis_size(axis), *array.shape))
    parts = lax.all_to_all(parts, axis, 0, 0, tiled=True)
    return parts.reshape(-1, array.shape[-1])


def traded(array, axis, bits):
    length = lax.axis_size(axis)
    return lax.ppermute(array, axis, [(i, i ^ bits) for i in range(length)])


def passed_along(array, axis, by):
    length = lax.axis_size(axis)
    pairs = [(i, i + by) for i in range(length) if 0 <= i + by < length]
    return lax.ppermute(array, axis, pairs)


def edges_of(now):
    return passed_along(now[:, -EDGE:], TM, 1), passed_along(now[:, :EDGE], TM, -1)


def lag_terms(now, edges, weights, first, last):
    before, after = edges
    hours = now.shape[1]
    wide = jnp.concatenate([before, now, after], axis=1)
    length = hours + EDGE
    resid = wide[:, EDGE:]
    for lag, weight in zip(LAGS, weights):
        resid = resid - weight[:, None] * wide[:, EDGE - lag : EDGE - lag + length]
    column = jnp.arange(length)
    inside = (~first | (column >= EDGE)) & (~last | (column < hours))
    resid = jnp.where(inside[None, :], resid, 0.0)
    back = None
    for lag, weight in zip(LAGS, weights):
        term = weight[:, None] * resid[:, lag : lag + hours]
        back = term if back is None else back + term
    return resid[:, :hours] - back


def dot(a, b):
    return jnp.dot(a, b, preferred_element_type=F32)


def by_hours(misfit, x_low):
    return lax.dot_general(misfit, x_low, (((1,), (1,)), ((), ())), preferred_element_type=F32)


def by_rows(f_low, misfit):
    return lax.dot_general(f_low, misfit, (((0,), (0,)), ((), ())), preferred_element_type=F32)


def add_up(total_ref, term, start_ref=None):
    start = 0.0 if start_ref is None else start_ref[...]
    total_ref[...] = jnp.where(pl.program_id(0) == 0, start, total_ref[...]) + term


def share_out(along, total_ref, pieces):
    @pl.when(pl.program_id(0) == pl.num_programs(0) - 1)
    def _():
        for k, piece in enumerate(pieces):
            size = piece.shape[0]
            start = pl.multiple_of((along ^ k) * size, size)
            piece[...] = total_ref[pl.ds(start, size), :]


def assembled(along, pieces, *outs):
    @pl.when(pl.program_id(0) == 0)
    def _():
        for k, piece in enumerate(pieces):
            size = piece.shape[0]
            start = pl.multiple_of((along ^ k) * size, size)
            for out in outs:
                out[pl.ds(start, size), :] = piece[...].astype(out.dtype)


def first_pass(place_ref, x_ref, f_ref, seen_ref, mask_ref, *refs):
    theirs_ref, mine_ref, kept_ref, *pieces, x_low_ref, total_ref = refs
    i = pl.program_id(0)

    @pl.when(i == 0)
    def _():
        x_low_ref[...] = x_ref[...].astype(BF16)

    x_low = x_low_ref[...]
    f_low = f_ref[...].astype(BF16)
    keep = mask_ref[...] != 0
    seen = seen_ref[...].astype(F32)
    misfit = jnp.where(keep, dot(f_low, x_low) - seen, 0.0).astype(BF16)
    kept_ref[...] = jnp.where(keep, seen, HIDDEN).astype(BF16)
    grad = by_hours(misfit, x_low)
    add_up(total_ref, by_rows(f_low, misfit))

    @pl.when(i < FIRST)
    def _():
        theirs_ref[...] = grad

    @pl.when(i >= FIRST)
    def _():
        mine_ref[...] = grad

    share_out(place_ref[1], total_ref, pieces)


def misfit_of(f_low, x_low, kept_ref):
    kept = kept_ref[...].astype(F32)
    return jnp.where(kept < HIDDEN / 2, dot(f_low, x_low) - kept, 0.0).astype(BF16)


def placed(place_ref, *refs):
    *came, x_ref, x_low_ref = refs
    assembled(place_ref[1], came, x_ref, x_low_ref)


def placed_low(place_ref, *refs):
    *came, x_low_ref = refs
    assembled(place_ref[1], came, x_low_ref)


def later_mine(_, x_low_ref, f_ref, kept_ref, grad_ref, total_ref):
    x_low = x_low_ref[...]
    f_low = f_ref[...].astype(BF16)
    misfit = misfit_of(f_low, x_low, kept_ref)
    grad_ref[...] = by_hours(misfit, x_low)
    add_up(total_ref, by_rows(f_low, misfit))


def later_theirs(_, x_low_ref, f_ref, kept_ref, grad_ref, misfit_ref):
    x_low = x_low_ref[...]
    misfit = misfit_of(f_ref[...].astype(BF16), x_low, kept_ref)
    misfit_ref[...] = misfit
    grad_ref[...] = by_hours(misfit, x_low)


def later_rows(place_ref, f_ref, misfit_ref, start_ref, *refs):
    *pieces, total_ref = refs
    add_up(total_ref, by_rows(f_ref[...].astype(BF16), misfit_ref[...]), start_ref)
    share_out(place_ref[1], total_ref, pieces)


def last_mine(_, x_low_ref, f_ref, f_out_ref, imputed_ref):
    f_out_ref[...] = f_ref[...]
    imputed_ref[...] = dot(f_ref[...].astype(BF16), x_low_ref[...]).astype(BF16)


def last_theirs(_, x_low_ref, f_ref, f_held_ref, imputed_held_ref, f_out_ref, imputed_ref):
    f_out_ref[...] = f_ref[...]
    imputed_ref[...] = dot(f_ref[...].astype(BF16), x_low_ref[...]).astype(BF16)


def half_pass(kernel, place, ins, outs, steps, limit, matmuls, scratch=(), aliases=()):
    maps = {
        "whole": lambda i, p: (0, 0),
        "half": lambda i, p: (i, 0),
        "mine": lambda i, p: (p[0] * steps + i, 0),
        "theirs": lambda i, p: ((1 - p[0]) * steps + i, 0),
        "both": lambda i, p: ((i // FIRST + 1 + p[0]) % 2 * FIRST + i % FIRST, 0),
        "all": lambda i, p: (i, 0),
        "lower": lambda i, p: (i, 0),
        "upper": lambda i, p: (steps + i, 0),
        "former": lambda i, p: (jnp.minimum(i, FIRST - 1), 0),
        "latter": lambda i, p: (jnp.maximum(i - FIRST, 0), 0),
    }
    tiles = {"whole": 1, "half": steps, "mine": 2 * steps, "theirs": 2 * steps}
    tiles.update(both=2 * FIRST, former=FIRST, latter=FIRST, all=steps)
    tiles.update(lower=2 * steps, upper=2 * steps)

    def spec(kind, shape):
        if kind == "held":
            return pl.BlockSpec(memory_space=pl.ANY)
        return pl.BlockSpec((shape[0] // tiles[kind], shape[1]), maps[kind])

    moved = sum(
        a.size * a.dtype.itemsize // (2 if k in ("mine", "theirs", "lower", "upper") else 1)
        for k, a in [*ins, *outs]
        if k != "held"
    )
    work = max(a.size for _, a in [*ins, *outs]) * 256 // 2
    return pl.pallas_call(
        kernel,
        out_shape=[s for _, s in outs],
        grid_spec=pltpu.PrefetchScalarGridSpec(
            num_scalar_prefetch=1,
            grid=(steps,),
            in_specs=[spec(k, a.shape) for k, a in ins],
            out_specs=[spec(k, s.shape) for k, s in outs],
            scratch_shapes=list(scratch),
        ),
        compiler_params=pltpu.CompilerParams(vmem_limit_bytes=limit * 2**20),
        cost_estimate=pl.CostEstimate(
            flops=2 * matmuls * work, bytes_accessed=moved, transcendentals=0
        ),
        input_output_aliases=dict(aliases),
        name=kernel.__name__,
    )(place, *[a for _, a in ins])


def local(observed, mask, series_factors, time_factors, ar_weights):
    rows, hours = observed.shape
    rank = time_factors.shape[0]
    hours_all = hours * lax.axis_size(TM)
    rows_all = rows * lax.axis_size(SERIES)
    step_f = rank / hours_all
    step_x = 1.0 / rows_all
    ridge_f = 0.1 * hours_all / rank
    ridge_x = 0.1 * rows_all
    lam = rows_all / 8.0

    half = rows // 2
    core = lax.axis_index(CORE)
    line = half // lax.axis_size(FAR)
    own_row = core * half + lax.axis_index(FAR) * line
    peers = lax.axis_size("x")
    band = rank // peers
    along = lax.axis_index("x")
    position = lax.axis_index(TM)
    first, last = position == 0, position == lax.axis_size(TM) - 1
    place = jnp.stack([core, along])

    def shape(n, m, dtype=F32):
        return jax.ShapeDtypeStruct((n, m), dtype)

    grad = ("half", shape(half, rank))
    flags = ("half", shape(half, hours, BF16))
    total = ("whole", shape(rank, hours))
    low = ("whole", shape(rank, hours, BF16))
    shares = [("whole", shape(band, hours))] * peers
    total_scratch = pltpu.VMEM((rank, hours), F32)
    low_scratch = pltpu.VMEM((rank, hours), BF16)
    f_part = lax.dynamic_slice_in_dim(series_factors, own_row, line, 0)
    x_part = lax.dynamic_slice_in_dim(time_factors, along * band, band, 0)
    w_part = lax.dynamic_slice_in_dim(ar_weights, along * band, band, 1)
    for sweep in range(ITERS):
        if sweep == 0:
            theirs, mine, kept, *parts = half_pass(
                first_pass,
                place,
                [("whole", time_factors), ("both", series_factors), ("both", observed), ("both", mask)],
                [("former", grad[1]), ("latter", grad[1]), ("all", shape(rows, hours, BF16)), *shares],
                2 * FIRST,
                58,
                6,
                [low_scratch, total_scratch],
            )
            came = lax.ppermute(theirs, CORE, SWAP)
        else:
            mine, start = half_pass(
                later_mine,
                place,
                [("whole", x_low), ("half", f_mine), ("upper", kept)],
                [grad, total],
                LATER,
                16,
                3,
            )
            f_theirs, mine, start = lax.optimization_barrier((f_theirs, mine, start))
            theirs, misfit = half_pass(
                later_theirs,
                place,
                [("whole", x_low), ("half", f_theirs), ("lower", kept)],
                [grad, flags],
                LATER,
                16,
                2,
            )
            came = lax.ppermute(theirs, CORE, SWAP)
            parts = half_pass(
                later_rows,
                place,
                [("half", f_theirs), ("half", misfit), ("whole", start)],
                shares,
                LATER,
                16,
                1,
                [total_scratch],
            )
        mine = mine + came
        mine, parts, x_part = lax.optimization_barrier((mine, parts, x_part))
        f_sum = scattered_sum(mine, FAR)
        received = [traded(parts[k], "x", k) for k in range(1, peers)]
        edge_x, received[0] = lax.optimization_barrier((x_part, received[0]))
        edges = edges_of(edge_x)
        x_sum = parts[0]
        for part in received:
            x_sum = x_sum + part
        lag = lag_terms(x_part, edges, w_part, first, last)
        f_part, x_sum, lag = lax.optimization_barrier((f_part, x_sum, lag))
        f_part = f_part - step_f * (f_sum + ridge_f * f_part)
        x_sum = x_sum + lax.ppermute(x_sum, "y_lo", SWAP)
        x_part = x_part - step_x * (x_sum + ridge_x * x_part + lam * lag)
        f_mine = gathered(f_part, FAR)
        pieces = [x_part] + [traded(x_part, "x", k) for k in range(1, peers)]
        *x_full, x_low = half_pass(
            placed if sweep + 1 == ITERS else placed_low,
            place,
            [("whole", p) for p in pieces],
            [total, low] if sweep + 1 == ITERS else [low],
            1,
            8,
            0,
        )
        f_mine, x_low = lax.optimization_barrier((f_mine, x_low))
        f_theirs = lax.ppermute(f_mine, CORE, SWAP)
    f_out, imputed = half_pass(
        last_mine,
        place,
        [("whole", x_low), ("half", f_mine)],
        [("mine", shape(rows, rank)), ("mine", shape(rows, hours, BF16))],
        LAST,
        16,
        1,
    )
    f_out, imputed = half_pass(
        last_theirs,
        place,
        [("whole", x_low), ("half", f_theirs), ("held", f_out), ("held", imputed)],
        [("theirs", shape(rows, rank)), ("theirs", shape(rows, hours, BF16))],
        LAST,
        16,
        1,
        aliases={3: 0, 4: 1},
    )
    return f_out, x_full[0], imputed


def solution(mesh):
    far = mesh.shape["tm"] // 4
    near = mesh.shape["series"] // 2
    split = Mesh(mesh.devices.reshape(near, 2, far, 2, 2), (*SERIES, *TM))
    in_specs = (P(SERIES, TM), P(SERIES, TM), P(SERIES, None), P(None, TM), P())
    out_specs = (P(SERIES, None), P(None, TM), P(SERIES, TM))
    return jax.shard_map(local, mesh=split, in_specs=in_specs, out_specs=out_specs, check_vma=False)
```

```python
import functools

import jax
import jax.numpy as jnp
from jax import lax
from jax.experimental import pallas as pl
from jax.experimental.pallas import tpu as pltpu
from jax.sharding import Mesh
from jax.sharding import PartitionSpec as P

ITERS = 2
LAGS = (1, 24, 168)
EDGE = 168
SERIES = ("x", "y_lo")
FAR = ("z", "y_hi")
CORE = "core"
TM = (*FAR, CORE)
SWAP = ((0, 1), (1, 0))
FIRST, LATER, LAST = 2, 1, 2
HIDDEN = 1e30
BF16, F32 = jnp.bfloat16, jnp.float32


def scattered_sum(array, axis):
    parts = array.reshape(lax.axis_size(axis), -1, array.shape[-1])
    return lax.all_to_all(parts, axis, 0, 0, tiled=True).sum(axis=0)


def gathered(array, axis):
    parts = jnp.broadcast_to(array[None], (lax.axis_size(axis), *array.shape))
    parts = lax.all_to_all(parts, axis, 0, 0, tiled=True)
    return parts.reshape(-1, array.shape[-1])


def traded(array, axis, bits):
    length = lax.axis_size(axis)
    return lax.ppermute(array, axis, [(i, i ^ bits) for i in range(length)])


def passed_along(array, axis, by):
    length = lax.axis_size(axis)
    pairs = [(i, i + by) for i in range(length) if 0 <= i + by < length]
    return lax.ppermute(array, axis, pairs)


def edges_of(now):
    return passed_along(now[:, -EDGE:], TM, 1), passed_along(now[:, :EDGE], TM, -1)


def lag_terms(now, edges, weights, first, last):
    before, after = edges
    hours = now.shape[1]
    wide = jnp.concatenate([before, now, after], axis=1)
    length = hours + EDGE
    resid = wide[:, EDGE:]
    for lag, weight in zip(LAGS, weights):
        resid = resid - weight[:, None] * wide[:, EDGE - lag : EDGE - lag + length]
    column = jnp.arange(length)
    inside = (~first | (column >= EDGE)) & (~last | (column < hours))
    resid = jnp.where(inside[None, :], resid, 0.0)
    back = None
    for lag, weight in zip(LAGS, weights):
        term = weight[:, None] * resid[:, lag : lag + hours]
        back = term if back is None else back + term
    return resid[:, :hours] - back


def dot(a, b):
    return jnp.dot(a, b, preferred_element_type=F32)


def by_hours(misfit, x_low):
    return lax.dot_general(misfit, x_low, (((1,), (1,)), ((), ())), preferred_element_type=F32)


def by_rows(f_low, misfit):
    return lax.dot_general(f_low, misfit, (((0,), (0,)), ((), ())), preferred_element_type=F32)


def add_up(total_ref, term, start_ref=None):
    start = 0.0 if start_ref is None else start_ref[...]
    total_ref[...] = jnp.where(pl.program_id(0) == 0, start, total_ref[...]) + term


def share_out(along, total_ref, pieces):
    @pl.when(pl.program_id(0) == pl.num_programs(0) - 1)
    def _():
        for k, piece in enumerate(pieces):
            size = piece.shape[0]
            start = pl.multiple_of((along ^ k) * size, size)
            piece[...] = total_ref[pl.ds(start, size), :]


def assembled(along, pieces, *outs):
    @pl.when(pl.program_id(0) == 0)
    def _():
        for k, piece in enumerate(pieces):
            size = piece.shape[0]
            start = pl.multiple_of((along ^ k) * size, size)
            for out in outs:
                out[pl.ds(start, size), :] = piece[...].astype(out.dtype)


def first_pass(_, along_ref, x_ref, f_ref, seen_ref, mask_ref, *refs):
    theirs_ref, mine_ref, kept_ref, *pieces, x_low_ref, total_ref = refs
    i = pl.program_id(0)

    @pl.when(i == 0)
    def _():
        x_low_ref[...] = x_ref[...].astype(BF16)

    x_low = x_low_ref[...]
    f_low = f_ref[...].astype(BF16)
    keep = mask_ref[...] != 0
    seen = seen_ref[...].astype(F32)
    misfit = jnp.where(keep, dot(f_low, x_low) - seen, 0.0).astype(BF16)
    kept_ref[...] = jnp.where(keep, seen, HIDDEN).astype(BF16)
    grad = by_hours(misfit, x_low)
    add_up(total_ref, by_rows(f_low, misfit))

    @pl.when(i < FIRST)
    def _():
        theirs_ref[...] = grad

    @pl.when(i >= FIRST)
    def _():
        mine_ref[...] = grad

    share_out(along_ref[0], total_ref, pieces)


def misfit_of(f_low, x_low, kept_ref):
    kept = kept_ref[...].astype(F32)
    return jnp.where(kept < HIDDEN / 2, dot(f_low, x_low) - kept, 0.0).astype(BF16)


def placed(_, along_ref, *refs):
    *came, x_ref, x_low_ref = refs
    assembled(along_ref[0], came, x_ref, x_low_ref)


def placed_low(_, along_ref, *refs):
    *came, x_low_ref = refs
    assembled(along_ref[0], came, x_low_ref)


def later_mine(_, __, x_low_ref, f_ref, kept_ref, grad_ref, total_ref):
    x_low = x_low_ref[...]
    f_low = f_ref[...].astype(BF16)
    misfit = misfit_of(f_low, x_low, kept_ref)
    grad_ref[...] = by_hours(misfit, x_low)
    add_up(total_ref, by_rows(f_low, misfit))


def later_theirs(_, __, x_low_ref, f_ref, kept_ref, grad_ref, misfit_ref):
    x_low = x_low_ref[...]
    misfit = misfit_of(f_ref[...].astype(BF16), x_low, kept_ref)
    misfit_ref[...] = misfit
    grad_ref[...] = by_hours(misfit, x_low)


def later_rows(_, along_ref, f_ref, misfit_ref, start_ref, *refs):
    *pieces, total_ref = refs
    add_up(total_ref, by_rows(f_ref[...].astype(BF16), misfit_ref[...]), start_ref)
    share_out(along_ref[0], total_ref, pieces)


def last_mine(_, __, x_low_ref, f_ref, f_out_ref, imputed_ref):
    f_out_ref[...] = f_ref[...]
    imputed_ref[...] = dot(f_ref[...].astype(BF16), x_low_ref[...]).astype(BF16)


def last_theirs(_, __, x_low_ref, f_ref, f_held_ref, imputed_held_ref, f_out_ref, imputed_ref):
    f_out_ref[...] = f_ref[...]
    imputed_ref[...] = dot(f_ref[...].astype(BF16), x_low_ref[...]).astype(BF16)


def half_pass(kernel, place, ins, outs, steps, limit, matmuls, scratch=(), aliases=()):
    maps = {
        "whole": lambda i, p, _: (0, 0),
        "half": lambda i, p, _: (i, 0),
        "mine": lambda i, p, _: (p[0] * steps + i, 0),
        "theirs": lambda i, p, _: ((1 - p[0]) * steps + i, 0),
        "both": lambda i, p, _: ((i // FIRST + 1 + p[0]) % 2 * FIRST + i % FIRST, 0),
        "all": lambda i, p, _: (i, 0),
        "lower": lambda i, p, _: (i, 0),
        "upper": lambda i, p, _: (steps + i, 0),
        "former": lambda i, p, _: (jnp.minimum(i, FIRST - 1), 0),
        "latter": lambda i, p, _: (jnp.maximum(i - FIRST, 0), 0),
    }
    tiles = {"whole": 1, "half": steps, "mine": 2 * steps, "theirs": 2 * steps}
    tiles.update(both=2 * FIRST, former=FIRST, latter=FIRST, all=steps)
    tiles.update(lower=2 * steps, upper=2 * steps)

    def spec(kind, shape):
        if kind == "held":
            return pl.BlockSpec(memory_space=pl.ANY)
        return pl.BlockSpec((shape[0] // tiles[kind], shape[1]), maps[kind])

    moved = sum(
        a.size * a.dtype.itemsize // (2 if k in ("mine", "theirs", "lower", "upper") else 1)
        for k, a in [*ins, *outs]
        if k != "held"
    )
    work = max(a.size for _, a in [*ins, *outs]) * 256 // 2
    return pl.pallas_call(
        kernel,
        out_shape=[s for _, s in outs],
        grid_spec=pltpu.PrefetchScalarGridSpec(
            num_scalar_prefetch=2,
            grid=(steps,),
            in_specs=[spec(k, a.shape) for k, a in ins],
            out_specs=[spec(k, s.shape) for k, s in outs],
            scratch_shapes=list(scratch),
        ),
        compiler_params=pltpu.CompilerParams(vmem_limit_bytes=limit * 2**20),
        cost_estimate=pl.CostEstimate(
            flops=2 * matmuls * work, bytes_accessed=moved, transcendentals=0
        ),
        input_output_aliases=dict(aliases),
        name=kernel.__name__,
    )(*place, *[a for _, a in ins])


def local(observed, mask, series_factors, time_factors, ar_weights):
    rows, hours = observed.shape
    rank = time_factors.shape[0]
    hours_all = hours * lax.axis_size(TM)
    rows_all = rows * lax.axis_size(SERIES)
    step_f = rank / hours_all
    step_x = 1.0 / rows_all
    ridge_f = 0.1 * hours_all / rank
    ridge_x = 0.1 * rows_all
    lam = rows_all / 8.0

    half = rows // 2
    core = lax.axis_index(CORE)
    line = half // lax.axis_size(FAR)
    own_row = core * half + lax.axis_index(FAR) * line
    peers = lax.axis_size("x")
    band = rank // peers
    along = lax.axis_index("x")
    position = lax.axis_index(TM)
    first, last = position == 0, position == lax.axis_size(TM) - 1
    place = (core.reshape(1), along.reshape(1))

    def shape(n, m, dtype=F32):
        return jax.ShapeDtypeStruct((n, m), dtype)

    grad = ("half", shape(half, rank))
    flags = ("half", shape(half, hours, BF16))
    total = ("whole", shape(rank, hours))
    low = ("whole", shape(rank, hours, BF16))
    shares = [("whole", shape(band, hours))] * peers
    total_scratch = pltpu.VMEM((rank, hours), F32)
    low_scratch = pltpu.VMEM((rank, hours), BF16)
    f_part = lax.dynamic_slice_in_dim(series_factors, own_row, line, 0)
    x_part = lax.dynamic_slice_in_dim(time_factors, along * band, band, 0)
    w_part = lax.dynamic_slice_in_dim(ar_weights, along * band, band, 1)
    for sweep in range(ITERS):
        if sweep == 0:
            theirs, mine, kept, *parts = half_pass(
                first_pass,
                place,
                [("whole", time_factors), ("both", series_factors), ("both", observed), ("both", mask)],
                [("former", grad[1]), ("latter", grad[1]), ("all", shape(rows, hours, BF16)), *shares],
                2 * FIRST,
                58,
                6,
                [low_scratch, total_scratch],
            )
            came = lax.ppermute(theirs, CORE, SWAP)
        else:
            mine, start = half_pass(
                later_mine,
                place,
                [("whole", x_low), ("half", f_mine), ("upper", kept)],
                [grad, total],
                LATER,
                16,
                3,
            )
            f_theirs, mine, start = lax.optimization_barrier((f_theirs, mine, start))
            theirs, misfit = half_pass(
                later_theirs,
                place,
                [("whole", x_low), ("half", f_theirs), ("lower", kept)],
                [grad, flags],
                LATER,
                16,
                2,
            )
            came = lax.ppermute(theirs, CORE, SWAP)
            parts = half_pass(
                later_rows,
                place,
                [("half", f_theirs), ("half", misfit), ("whole", start)],
                shares,
                LATER,
                16,
                1,
                [total_scratch],
            )
        mine = mine + came
        mine, parts, x_part = lax.optimization_barrier((mine, parts, x_part))
        f_sum = scattered_sum(mine, FAR)
        received = [traded(parts[k], "x", k) for k in range(1, peers)]
        edge_x, received[0] = lax.optimization_barrier((x_part, received[0]))
        edges = edges_of(edge_x)
        x_sum = parts[0]
        for part in received:
            x_sum = x_sum + part
        lag = lag_terms(x_part, edges, w_part, first, last)
        f_part, x_sum, lag = lax.optimization_barrier((f_part, x_sum, lag))
        f_part = f_part - step_f * (f_sum + ridge_f * f_part)
        x_sum = x_sum + lax.ppermute(x_sum, "y_lo", SWAP)
        x_part = x_part - step_x * (x_sum + ridge_x * x_part + lam * lag)
        f_mine = gathered(f_part, FAR)
        pieces = [x_part] + [traded(x_part, "x", k) for k in range(1, peers)]
        *x_full, x_low = half_pass(
            placed if sweep + 1 == ITERS else placed_low,
            place,
            [("whole", p) for p in pieces],
            [total, low] if sweep + 1 == ITERS else [low],
            1,
            8,
            0,
        )
        f_mine, x_low = lax.optimization_barrier((f_mine, x_low))
        f_theirs = lax.ppermute(f_mine, CORE, SWAP)
    f_out, imputed = half_pass(
        last_mine,
        place,
        [("whole", x_low), ("half", f_mine)],
        [("mine", shape(rows, rank)), ("mine", shape(rows, hours, BF16))],
        LAST,
        16,
        1,
    )
    f_out, imputed = half_pass(
        last_theirs,
        place,
        [("whole", x_low), ("half", f_theirs), ("held", f_out), ("held", imputed)],
        [("theirs", shape(rows, rank)), ("theirs", shape(rows, hours, BF16))],
        LAST,
        16,
        1,
        aliases={4: 0, 5: 1},
    )
    return f_out, x_full[0], imputed


def solution(mesh):
    far = mesh.shape["tm"] // 4
    near = mesh.shape["series"] // 2
    split = Mesh(mesh.devices.reshape(near, 2, far, 2, 2), (*SERIES, *TM))
    in_specs = (P(SERIES, TM), P(SERIES, TM), P(SERIES, None), P(None, TM), P())
    out_specs = (P(SERIES, None), P(None, TM), P(SERIES, TM))
    return jax.shard_map(local, mesh=split, in_specs=in_specs, out_specs=out_specs, check_vma=False)
```

```python
import functools

import jax
import jax.numpy as jnp
from jax import lax
from jax.experimental import pallas as pl
from jax.experimental.pallas import tpu as pltpu
from jax.sharding import Mesh
from jax.sharding import PartitionSpec as P

ITERS = 2
LAGS = (1, 24, 168)
EDGE = 168
SERIES = ("x", "y_lo")
FAR = ("z", "y_hi")
CORE = "core"
TM = (*FAR, CORE)
SWAP = ((0, 1), (1, 0))
FIRST, LATER, LAST = 2, 1, 2
HIDDEN = 1e30
BF16, F32 = jnp.bfloat16, jnp.float32


def scattered_sum(array, axis):
    parts = array.reshape(lax.axis_size(axis), -1, array.shape[-1])
    return lax.all_to_all(parts, axis, 0, 0, tiled=True).sum(axis=0)


def gathered(array, axis):
    parts = jnp.broadcast_to(array[None], (lax.axis_size(axis), *array.shape))
    parts = lax.all_to_all(parts, axis, 0, 0, tiled=True)
    return parts.reshape(-1, array.shape[-1])


def traded(array, axis, bits):
    length = lax.axis_size(axis)
    return lax.ppermute(array, axis, [(i, i ^ bits) for i in range(length)])


def passed_along(array, axis, by):
    length = lax.axis_size(axis)
    pairs = [(i, i + by) for i in range(length) if 0 <= i + by < length]
    return lax.ppermute(array, axis, pairs)


def edges_of(now):
    return passed_along(now[:, -EDGE:], TM, 1), passed_along(now[:, :EDGE], TM, -1)


def lag_terms(now, edges, weights, first, last):
    before, after = edges
    hours = now.shape[1]
    wide = jnp.concatenate([before, now, after], axis=1)
    length = hours + EDGE
    resid = wide[:, EDGE:]
    for lag, weight in zip(LAGS, weights):
        resid = resid - weight[:, None] * wide[:, EDGE - lag : EDGE - lag + length]
    column = jnp.arange(length)
    inside = (~first | (column >= EDGE)) & (~last | (column < hours))
    resid = jnp.where(inside[None, :], resid, 0.0)
    back = None
    for lag, weight in zip(LAGS, weights):
        term = weight[:, None] * resid[:, lag : lag + hours]
        back = term if back is None else back + term
    return resid[:, :hours] - back


def dot(a, b):
    return jnp.dot(a, b, preferred_element_type=F32)


def by_hours(misfit, x_low):
    return lax.dot_general(misfit, x_low, (((1,), (1,)), ((), ())), preferred_element_type=F32)


def by_rows(f_low, misfit):
    return lax.dot_general(f_low, misfit, (((0,), (0,)), ((), ())), preferred_element_type=F32)


def add_up(total_ref, term, start_ref=None):
    start = 0.0 if start_ref is None else start_ref[...]
    total_ref[...] = jnp.where(pl.program_id(0) == 0, start, total_ref[...]) + term


def share_out(along, total_ref, pieces):
    @pl.when(pl.program_id(0) == pl.num_programs(0) - 1)
    def _():
        for k, piece in enumerate(pieces):
            size = piece.shape[0]
            start = pl.multiple_of((along ^ k) * size, size)
            piece[...] = total_ref[pl.ds(start, size), :]


def assembled(along, pieces, *outs):
    @pl.when(pl.program_id(0) == 0)
    def _():
        for k, piece in enumerate(pieces):
            size = piece.shape[0]
            start = pl.multiple_of((along ^ k) * size, size)
            for out in outs:
                out[pl.ds(start, size), :] = piece[...].astype(out.dtype)


def first_pass(_, along_ref, x_ref, f_ref, seen_ref, mask_ref, *refs):
    theirs_ref, mine_ref, kept_ref, *pieces, x_low_ref, total_ref = refs
    i = pl.program_id(0)

    @pl.when(i == 0)
    def _():
        x_low_ref[...] = x_ref[...].astype(BF16)

    x_low = x_low_ref[...]
    f_low = f_ref[...].astype(BF16)
    keep = mask_ref[...] != 0
    seen = seen_ref[...].astype(F32)
    misfit = jnp.where(keep, dot(f_low, x_low) - seen, 0.0).astype(BF16)
    kept_ref[...] = jnp.where(keep, seen, HIDDEN).astype(BF16)
    grad = by_hours(misfit, x_low)
    add_up(total_ref, by_rows(f_low, misfit))

    @pl.when(i < FIRST)
    def _():
        theirs_ref[...] = grad

    @pl.when(i >= FIRST)
    def _():
        mine_ref[...] = grad

    share_out(along_ref[0], total_ref, pieces)


def misfit_of(f_low, x_low, kept_ref):
    kept = kept_ref[...].astype(F32)
    return jnp.where(kept < HIDDEN / 2, dot(f_low, x_low) - kept, 0.0).astype(BF16)


def placed(along_ref, *refs):
    *came, x_ref, x_low_ref = refs
    assembled(along_ref[0], came, x_ref, x_low_ref)


def placed_low(along_ref, *refs):
    *came, x_low_ref = refs
    assembled(along_ref[0], came, x_low_ref)


def later_mine(x_low_ref, f_ref, kept_ref, grad_ref, total_ref):
    x_low = x_low_ref[...]
    f_low = f_ref[...].astype(BF16)
    misfit = misfit_of(f_low, x_low, kept_ref)
    grad_ref[...] = by_hours(misfit, x_low)
    add_up(total_ref, by_rows(f_low, misfit))


def later_theirs(x_low_ref, f_ref, kept_ref, grad_ref, misfit_ref):
    x_low = x_low_ref[...]
    misfit = misfit_of(f_ref[...].astype(BF16), x_low, kept_ref)
    misfit_ref[...] = misfit
    grad_ref[...] = by_hours(misfit, x_low)


def later_rows(along_ref, f_ref, misfit_ref, start_ref, *refs):
    *pieces, total_ref = refs
    add_up(total_ref, by_rows(f_ref[...].astype(BF16), misfit_ref[...]), start_ref)
    share_out(along_ref[0], total_ref, pieces)


def last_mine(_, x_low_ref, f_ref, f_out_ref, imputed_ref):
    f_out_ref[...] = f_ref[...]
    imputed_ref[...] = dot(f_ref[...].astype(BF16), x_low_ref[...]).astype(BF16)


def last_theirs(_, x_low_ref, f_ref, f_held_ref, imputed_held_ref, f_out_ref, imputed_ref):
    f_out_ref[...] = f_ref[...]
    imputed_ref[...] = dot(f_ref[...].astype(BF16), x_low_ref[...]).astype(BF16)


def half_pass(kernel, place, ins, outs, steps, limit, matmuls, scratch=(), aliases=()):
    maps = {
        "whole": lambda i, *p: (0, 0),
        "half": lambda i, *p: (i, 0),
        "mine": lambda i, *p: (p[0][0] * steps + i, 0),
        "theirs": lambda i, *p: ((1 - p[0][0]) * steps + i, 0),
        "both": lambda i, *p: ((i // FIRST + 1 + p[0][0]) % 2 * FIRST + i % FIRST, 0),
        "all": lambda i, *p: (i, 0),
        "lower": lambda i, *p: (i, 0),
        "upper": lambda i, *p: (steps + i, 0),
        "former": lambda i, *p: (jnp.minimum(i, FIRST - 1), 0),
        "latter": lambda i, *p: (jnp.maximum(i - FIRST, 0), 0),
    }
    tiles = {"whole": 1, "half": steps, "mine": 2 * steps, "theirs": 2 * steps}
    tiles.update(both=2 * FIRST, former=FIRST, latter=FIRST, all=steps)
    tiles.update(lower=2 * steps, upper=2 * steps)

    def spec(kind, shape):
        if kind == "held":
            return pl.BlockSpec(memory_space=pl.ANY)
        return pl.BlockSpec((shape[0] // tiles[kind], shape[1]), maps[kind])

    moved = sum(
        a.size * a.dtype.itemsize // (2 if k in ("mine", "theirs", "lower", "upper") else 1)
        for k, a in [*ins, *outs]
        if k != "held"
    )
    work = max(a.size for _, a in [*ins, *outs]) * 256 // 2
    return pl.pallas_call(
        kernel,
        out_shape=[s for _, s in outs],
        grid_spec=pltpu.PrefetchScalarGridSpec(
            num_scalar_prefetch=len(place),
            grid=(steps,),
            in_specs=[spec(k, a.shape) for k, a in ins],
            out_specs=[spec(k, s.shape) for k, s in outs],
            scratch_shapes=list(scratch),
        ),
        compiler_params=pltpu.CompilerParams(vmem_limit_bytes=limit * 2**20),
        cost_estimate=pl.CostEstimate(
            flops=2 * matmuls * work, bytes_accessed=moved, transcendentals=0
        ),
        input_output_aliases=dict(aliases),
        name=kernel.__name__,
    )(*place, *[a for _, a in ins])


def local(observed, mask, series_factors, time_factors, ar_weights):
    rows, hours = observed.shape
    rank = time_factors.shape[0]
    hours_all = hours * lax.axis_size(TM)
    rows_all = rows * lax.axis_size(SERIES)
    step_f = rank / hours_all
    step_x = 1.0 / rows_all
    ridge_f = 0.1 * hours_all / rank
    ridge_x = 0.1 * rows_all
    lam = rows_all / 8.0

    half = rows // 2
    core = lax.axis_index(CORE)
    line = half // lax.axis_size(FAR)
    own_row = core * half + lax.axis_index(FAR) * line
    peers = lax.axis_size("x")
    band = rank // peers
    along = lax.axis_index("x")
    position = lax.axis_index(TM)
    first, last = position == 0, position == lax.axis_size(TM) - 1
    which_core, which_place = core.reshape(1), along.reshape(1)

    def shape(n, m, dtype=F32):
        return jax.ShapeDtypeStruct((n, m), dtype)

    grad = ("half", shape(half, rank))
    flags = ("half", shape(half, hours, BF16))
    total = ("whole", shape(rank, hours))
    low = ("whole", shape(rank, hours, BF16))
    shares = [("whole", shape(band, hours))] * peers
    total_scratch = pltpu.VMEM((rank, hours), F32)
    low_scratch = pltpu.VMEM((rank, hours), BF16)
    f_part = lax.dynamic_slice_in_dim(series_factors, own_row, line, 0)
    x_part = lax.dynamic_slice_in_dim(time_factors, along * band, band, 0)
    w_part = lax.dynamic_slice_in_dim(ar_weights, along * band, band, 1)
    for sweep in range(ITERS):
        if sweep == 0:
            theirs, mine, kept, *parts = half_pass(
                first_pass,
                (which_core, which_place),
                [("whole", time_factors), ("both", series_factors), ("both", observed), ("both", mask)],
                [("former", grad[1]), ("latter", grad[1]), ("all", shape(rows, hours, BF16)), *shares],
                2 * FIRST,
                58,
                6,
                [low_scratch, total_scratch],
            )
            came = lax.ppermute(theirs, CORE, SWAP)
        else:
            mine, start = half_pass(
                later_mine,
                (),
                [("whole", x_low), ("half", f_mine), ("upper", kept)],
                [grad, total],
                LATER,
                16,
                3,
            )
            f_theirs, mine, start = lax.optimization_barrier((f_theirs, mine, start))
            theirs, misfit = half_pass(
                later_theirs,
                (),
                [("whole", x_low), ("half", f_theirs), ("lower", kept)],
                [grad, flags],
                LATER,
                16,
                2,
            )
            came = lax.ppermute(theirs, CORE, SWAP)
            parts = half_pass(
                later_rows,
                (which_place,),
                [("half", f_theirs), ("half", misfit), ("whole", start)],
                shares,
                LATER,
                16,
                1,
                [total_scratch],
            )
        mine = mine + came
        mine, parts, x_part = lax.optimization_barrier((mine, parts, x_part))
        f_sum = scattered_sum(mine, FAR)
        received = [traded(parts[k], "x", k) for k in range(1, peers)]
        edge_x, received[0] = lax.optimization_barrier((x_part, received[0]))
        edges = edges_of(edge_x)
        x_sum = parts[0]
        for part in received:
            x_sum = x_sum + part
        lag = lag_terms(x_part, edges, w_part, first, last)
        f_part, x_sum, lag = lax.optimization_barrier((f_part, x_sum, lag))
        f_part = f_part - step_f * (f_sum + ridge_f * f_part)
        x_sum = x_sum + lax.ppermute(x_sum, "y_lo", SWAP)
        x_part = x_part - step_x * (x_sum + ridge_x * x_part + lam * lag)
        f_mine = gathered(f_part, FAR)
        pieces = [x_part] + [traded(x_part, "x", k) for k in range(1, peers)]
        *x_full, x_low = half_pass(
            placed if sweep + 1 == ITERS else placed_low,
            (which_place,),
            [("whole", p) for p in pieces],
            [total, low] if sweep + 1 == ITERS else [low],
            1,
            8,
            0,
        )
        f_mine, x_low = lax.optimization_barrier((f_mine, x_low))
        f_theirs = lax.ppermute(f_mine, CORE, SWAP)
    f_out, imputed = half_pass(
        last_mine,
        (which_core,),
        [("whole", x_low), ("half", f_mine)],
        [("mine", shape(rows, rank)), ("mine", shape(rows, hours, BF16))],
        LAST,
        16,
        1,
    )
    f_out, imputed = half_pass(
        last_theirs,
        (which_core,),
        [("whole", x_low), ("half", f_theirs), ("held", f_out), ("held", imputed)],
        [("theirs", shape(rows, rank)), ("theirs", shape(rows, hours, BF16))],
        LAST,
        16,
        1,
        aliases={3: 0, 4: 1},
    )
    return f_out, x_full[0], imputed


def solution(mesh):
    far = mesh.shape["tm"] // 4
    near = mesh.shape["series"] // 2
    split = Mesh(mesh.devices.reshape(near, 2, far, 2, 2), (*SERIES, *TM))
    in_specs = (P(SERIES, TM), P(SERIES, TM), P(SERIES, None), P(None, TM), P())
    out_specs = (P(SERIES, None), P(None, TM), P(SERIES, TM))
    return jax.shard_map(local, mesh=split, in_specs=in_specs, out_specs=out_specs, check_vma=False)
```

```python
import functools

import jax
import jax.numpy as jnp
from jax import lax
from jax.experimental import pallas as pl
from jax.experimental.pallas import tpu as pltpu
from jax.sharding import Mesh
from jax.sharding import PartitionSpec as P

ITERS = 2
LAGS = (1, 24, 168)
EDGE = 168
SERIES = ("x", "y_lo")
FAR = ("z", "y_hi")
CORE = "core"
TM = (*FAR, CORE)
SWAP = ((0, 1), (1, 0))
FIRST, LATER, LAST = 2, 1, 2
HIDDEN = 1e30
BF16, F32 = jnp.bfloat16, jnp.float32


def scattered_sum(array, axis):
    parts = array.reshape(lax.axis_size(axis), -1, array.shape[-1])
    return lax.all_to_all(parts, axis, 0, 0, tiled=True).sum(axis=0)


def gathered(array, axis):
    parts = jnp.broadcast_to(array[None], (lax.axis_size(axis), *array.shape))
    parts = lax.all_to_all(parts, axis, 0, 0, tiled=True)
    return parts.reshape(-1, array.shape[-1])


def traded(array, axis, bits):
    length = lax.axis_size(axis)
    return lax.ppermute(array, axis, [(i, i ^ bits) for i in range(length)])


def passed_along(array, axis, by):
    length = lax.axis_size(axis)
    pairs = [(i, i + by) for i in range(length) if 0 <= i + by < length]
    return lax.ppermute(array, axis, pairs)


def edges_of(now):
    return passed_along(now[:, -EDGE:], TM, 1), passed_along(now[:, :EDGE], TM, -1)


def lag_terms(now, edges, weights, first, last):
    before, after = edges
    hours = now.shape[1]
    wide = jnp.concatenate([before, now, after], axis=1)
    length = hours + EDGE
    resid = wide[:, EDGE:]
    for lag, weight in zip(LAGS, weights):
        resid = resid - weight[:, None] * wide[:, EDGE - lag : EDGE - lag + length]
    column = jnp.arange(length)
    inside = (~first | (column >= EDGE)) & (~last | (column < hours))
    resid = jnp.where(inside[None, :], resid, 0.0)
    back = None
    for lag, weight in zip(LAGS, weights):
        term = weight[:, None] * resid[:, lag : lag + hours]
        back = term if back is None else back + term
    return resid[:, :hours] - back


def dot(a, b):
    return jnp.dot(a, b, preferred_element_type=F32)


def by_hours(misfit, x_low):
    return lax.dot_general(misfit, x_low, (((1,), (1,)), ((), ())), preferred_element_type=F32)


def by_rows(f_low, misfit):
    return lax.dot_general(f_low, misfit, (((0,), (0,)), ((), ())), preferred_element_type=F32)


def add_up(total_ref, term, start_ref=None):
    start = 0.0 if start_ref is None else start_ref[...]
    total_ref[...] = jnp.where(pl.program_id(0) == 0, start, total_ref[...]) + term


def share_out(along, total_ref, pieces):
    @pl.when(pl.program_id(0) == pl.num_programs(0) - 1)
    def _():
        for k, piece in enumerate(pieces):
            size = piece.shape[0]
            start = pl.multiple_of((along ^ k) * size, size)
            piece[...] = total_ref[pl.ds(start, size), :]


def assembled(along, pieces, *outs):
    @pl.when(pl.program_id(0) == 0)
    def _():
        for k, piece in enumerate(pieces):
            size = piece.shape[0]
            start = pl.multiple_of((along ^ k) * size, size)
            for out in outs:
                out[pl.ds(start, size), :] = piece[...].astype(out.dtype)


def first_pass(_, along_ref, x_ref, f_ref, seen_ref, mask_ref, *refs):
    theirs_ref, mine_ref, kept_ref, *pieces, x_low_ref, total_ref = refs
    i = pl.program_id(0)

    @pl.when(i == 0)
    def _():
        x_low_ref[...] = x_ref[...].astype(BF16)

    x_low = x_low_ref[...]
    f_low = f_ref[...].astype(BF16)
    keep = mask_ref[...] != 0
    seen = seen_ref[...].astype(F32)
    misfit = jnp.where(keep, dot(f_low, x_low) - seen, 0.0).astype(BF16)
    kept_ref[...] = jnp.where(keep, seen, HIDDEN).astype(BF16)
    grad = by_hours(misfit, x_low)
    add_up(total_ref, by_rows(f_low, misfit))

    @pl.when(i < FIRST)
    def _():
        theirs_ref[...] = grad

    @pl.when(i >= FIRST)
    def _():
        mine_ref[...] = grad

    share_out(along_ref[0], total_ref, pieces)


def misfit_of(f_low, x_low, kept_ref):
    kept = kept_ref[...].astype(F32)
    return jnp.where(kept < HIDDEN / 2, dot(f_low, x_low) - kept, 0.0).astype(BF16)


def placed(_, along_ref, *refs):
    *came, x_ref, x_low_ref = refs
    assembled(along_ref[0], came, x_ref, x_low_ref)


def placed_low(_, along_ref, *refs):
    *came, x_low_ref = refs
    assembled(along_ref[0], came, x_low_ref)


def later_mine(_, __, x_low_ref, f_ref, kept_ref, grad_ref, total_ref):
    x_low = x_low_ref[...]
    f_low = f_ref[...].astype(BF16)
    misfit = misfit_of(f_low, x_low, kept_ref)
    grad_ref[...] = by_hours(misfit, x_low)
    add_up(total_ref, by_rows(f_low, misfit))


def later_theirs(_, __, x_low_ref, f_ref, kept_ref, grad_ref, misfit_ref):
    x_low = x_low_ref[...]
    misfit = misfit_of(f_ref[...].astype(BF16), x_low, kept_ref)
    misfit_ref[...] = misfit
    grad_ref[...] = by_hours(misfit, x_low)


def later_rows(_, along_ref, f_ref, misfit_ref, start_ref, *refs):
    *pieces, total_ref = refs
    add_up(total_ref, by_rows(f_ref[...].astype(BF16), misfit_ref[...]), start_ref)
    share_out(along_ref[0], total_ref, pieces)


def last_mine(_, __, x_low_ref, f_ref, f_out_ref, imputed_ref):
    f_out_ref[...] = f_ref[...]
    imputed_ref[...] = dot(f_ref[...].astype(BF16), x_low_ref[...]).astype(BF16)


def last_theirs(_, __, x_low_ref, f_ref, f_held_ref, imputed_held_ref, f_out_ref, imputed_ref):
    f_out_ref[...] = f_ref[...]
    imputed_ref[...] = dot(f_ref[...].astype(BF16), x_low_ref[...]).astype(BF16)


def half_pass(kernel, place, ins, outs, steps, limit, matmuls, scratch=(), aliases=()):
    maps = {
        "whole": lambda i, p, _: (0, 0),
        "half": lambda i, p, _: (i, 0),
        "mine": lambda i, p, _: (p[0] * steps + i, 0),
        "theirs": lambda i, p, _: ((1 - p[0]) * steps + i, 0),
        "both": lambda i, p, _: ((i // FIRST + 1 + p[0]) % 2 * FIRST + i % FIRST, 0),
        "all": lambda i, p, _: (i, 0),
        "lower": lambda i, p, _: (i, 0),
        "upper": lambda i, p, _: (steps + i, 0),
        "former": lambda i, p, _: (jnp.minimum(i, FIRST - 1), 0),
        "latter": lambda i, p, _: (jnp.maximum(i - FIRST, 0), 0),
    }
    tiles = {"whole": 1, "half": steps, "mine": 2 * steps, "theirs": 2 * steps}
    tiles.update(both=2 * FIRST, former=FIRST, latter=FIRST, all=steps)
    tiles.update(lower=2 * steps, upper=2 * steps)

    def spec(kind, shape):
        if kind == "held":
            return pl.BlockSpec(memory_space=pl.ANY)
        return pl.BlockSpec((shape[0] // tiles[kind], shape[1]), maps[kind])

    moved = sum(
        a.size * a.dtype.itemsize // (2 if k in ("mine", "theirs", "lower", "upper") else 1)
        for k, a in [*ins, *outs]
        if k != "held"
    )
    work = max(a.size for _, a in [*ins, *outs]) * 256 // 2
    return pl.pallas_call(
        kernel,
        out_shape=[s for _, s in outs],
        grid_spec=pltpu.PrefetchScalarGridSpec(
            num_scalar_prefetch=2,
            grid=(steps,),
            in_specs=[spec(k, a.shape) for k, a in ins],
            out_specs=[spec(k, s.shape) for k, s in outs],
            scratch_shapes=list(scratch),
        ),
        compiler_params=pltpu.CompilerParams(vmem_limit_bytes=limit * 2**20),
        cost_estimate=pl.CostEstimate(
            flops=2 * matmuls * work, bytes_accessed=moved, transcendentals=0
        ),
        input_output_aliases=dict(aliases),
        name=kernel.__name__,
    )(*place, *[a for _, a in ins])


def local(observed, mask, series_factors, time_factors, ar_weights):
    rows, hours = observed.shape
    rank = time_factors.shape[0]
    hours_all = hours * lax.axis_size(TM)
    rows_all = rows * lax.axis_size(SERIES)
    step_f = rank / hours_all
    step_x = 1.0 / rows_all
    ridge_f = 0.1 * hours_all / rank
    ridge_x = 0.1 * rows_all
    lam = rows_all / 8.0

    half = rows // 2
    core = lax.axis_index(CORE)
    line = half // lax.axis_size(FAR)
    own_row = core * half + lax.axis_index(FAR) * line
    peers = lax.axis_size("x")
    band = rank // peers
    along = lax.axis_index("x")
    position = lax.axis_index(TM)
    first, last = position == 0, position == lax.axis_size(TM) - 1
    place = (core.reshape(1), along.reshape(1))

    def shape(n, m, dtype=F32):
        return jax.ShapeDtypeStruct((n, m), dtype)

    grad = ("half", shape(half, rank))
    flags = ("half", shape(half, hours, BF16))
    total = ("whole", shape(rank, hours))
    low = ("whole", shape(rank, hours, BF16))
    shares = [("whole", shape(band, hours))] * peers
    total_scratch = pltpu.VMEM((rank, hours), F32)
    low_scratch = pltpu.VMEM((rank, hours), BF16)
    f_part = lax.dynamic_slice_in_dim(series_factors, own_row, line, 0)
    x_part = lax.dynamic_slice_in_dim(time_factors, along * band, band, 0)
    w_part = lax.dynamic_slice_in_dim(ar_weights, along * band, band, 1)
    for sweep in range(ITERS):
        if sweep == 0:
            theirs, mine, kept, *parts = half_pass(
                first_pass,
                place,
                [("whole", time_factors), ("both", series_factors), ("both", observed), ("both", mask)],
                [("former", grad[1]), ("latter", grad[1]), ("all", shape(rows, hours, BF16)), *shares],
                2 * FIRST,
                58,
                6,
                [low_scratch, total_scratch],
            )
            came = lax.ppermute(theirs, CORE, SWAP)
        else:
            mine, start = half_pass(
                later_mine,
                place,
                [("whole", x_low), ("half", f_mine), ("upper", kept)],
                [grad, total],
                LATER,
                16,
                3,
            )
            f_theirs, mine, start = lax.optimization_barrier((f_theirs, mine, start))
            theirs, misfit = half_pass(
                later_theirs,
                place,
                [("whole", x_low), ("half", f_theirs), ("lower", kept)],
                [grad, flags],
                LATER,
                16,
                2,
            )
            came = lax.ppermute(theirs, CORE, SWAP)
            parts = half_pass(
                later_rows,
                place,
                [("half", f_theirs), ("half", misfit), ("whole", start)],
                shares,
                LATER,
                16,
                1,
                [total_scratch],
            )
        mine = mine + came
        mine, parts, x_part = lax.optimization_barrier((mine, parts, x_part))
        f_sum = scattered_sum(mine, FAR)
        received = [traded(parts[k], "x", k) for k in range(1, peers)]
        edges = edges_of(x_part)
        x_sum = parts[0]
        for part in received:
            x_sum = x_sum + part
        f_part, x_sum, edges = lax.optimization_barrier((f_part, x_sum, edges))
        lag = lag_terms(x_part, edges, w_part, first, last)
        f_part = f_part - step_f * (f_sum + ridge_f * f_part)
        x_sum = x_sum + lax.ppermute(x_sum, "y_lo", SWAP)
        x_part = x_part - step_x * (x_sum + ridge_x * x_part + lam * lag)
        f_mine = gathered(f_part, FAR)
        pieces = [x_part] + [traded(x_part, "x", k) for k in range(1, peers)]
        *x_full, x_low = half_pass(
            placed if sweep + 1 == ITERS else placed_low,
            place,
            [("whole", p) for p in pieces],
            [total, low] if sweep + 1 == ITERS else [low],
            1,
            8,
            0,
        )
        f_mine, x_low = lax.optimization_barrier((f_mine, x_low))
        f_theirs = lax.ppermute(f_mine, CORE, SWAP)
    f_out, imputed = half_pass(
        last_mine,
        place,
        [("whole", x_low), ("half", f_mine)],
        [("mine", shape(rows, rank)), ("mine", shape(rows, hours, BF16))],
        LAST,
        16,
        1,
    )
    f_out, imputed = half_pass(
        last_theirs,
        place,
        [("whole", x_low), ("half", f_theirs), ("held", f_out), ("held", imputed)],
        [("theirs", shape(rows, rank)), ("theirs", shape(rows, hours, BF16))],
        LAST,
        16,
        1,
        aliases={4: 0, 5: 1},
    )
    return f_out, x_full[0], imputed


def solution(mesh):
    far = mesh.shape["tm"] // 4
    near = mesh.shape["series"] // 2
    split = Mesh(mesh.devices.reshape(near, 2, far, 2, 2), (*SERIES, *TM))
    in_specs = (P(SERIES, TM), P(SERIES, TM), P(SERIES, None), P(None, TM), P())
    out_specs = (P(SERIES, None), P(None, TM), P(SERIES, TM))
    return jax.shard_map(local, mesh=split, in_specs=in_specs, out_specs=out_specs, check_vma=False)
```
